32 devices in a mesh: depth: 16 (over z, x, core), lat: 2 (over y).
Axes of the slice: x: 2, y: 2, z: 4, core: 2. Of those that a mesh axis runs over, the one named last changes fastest.
Arguments:
- in_flight: float32 [16, 4, 64, 256], P('depth', None, 'lat'), may hold values from -6 to 6
- entering: float32 [2, 4, 64, 256], P(None, None, 'lat'), may hold values from -6 to 6
- classes: int32 [16, 64, 256], P('depth', 'lat'), may hold values from 0 to 31
- freq_phase: float32 [18], replicated, may hold values from 4 to 8.5
- class_slowness: float32 [32], replicated, may hold values from 0.8 to 1.4
Outputs:
- images: float32 [16, 8, 64, 256], P('depth', None, 'lat')
- wave_out: float32 [16, 4, 64, 256], P('depth', None, 'lat')
The draws below stay inside these ranges and needn't reach their ends.
All inputs are finite; a program needn't handle non-finite values.
Results may differ from the reference program's by a relative error of at most 0.0003.
Values sent between devices are 32-bit elements; how exact they have to be, the bound alone decides.
No kernel may reach another device: no remote copies, remote signals or barrier semaphores. Data moves between devices by JAX's collectives and lax.ppermute only.
A program may use at most 64 MiB of HBM per device.

```python
import math
import jax
import jax.numpy as jnp
from jax import lax

NX = 256
TERMS = 16
OFFSETS = 8
CLASSES = 32
TURNS = 3
NZ = 16
NY = 64
FREQS = 18


def plant(values, key, smallest, top_value):
    longest = values.shape.index(max(values.shape))
    spots = []
    for shift in (0, 1):
        where = [jax.random.randint(jax.random.fold_in(key, axis), (), 0, length) for axis, length in enumerate(values.shape)]
        where[longest] = (where[longest] + shift) % values.shape[longest]
        spots.append(tuple(where))
    return values.at[spots[0]].set(smallest).at[spots[1]].set(top_value)


def steps_of(stream_key, dims, shards, smallest, high):
    def one(position, blocks):
        draws = jax.random.uniform(jax.random.fold_in(jax.random.fold_in(stream_key, 6), position), (blocks,), jnp.float32, smallest / len(shards), high / len(shards))
        return jnp.repeat(jnp.exp(draws), dims[position] // blocks).reshape((-1,) + (1,) * (len(dims) - position - 1))

    loudness = one(*shards[0])
    for cut in shards[1:]:
        loudness = loudness * one(*cut)
    return loudness


def noise(own_key, extent, spread, bound, shards=(), kind=jnp.bfloat16):
    loudness = steps_of(own_key, extent, shards, -0.22, 0.18) if shards else 1.0
    values = jax.random.normal(own_key, extent, jnp.float32) * spread * loudness
    return jnp.minimum(jnp.maximum(values, -bound), bound).astype(kind)


def setup_inputs(seed: int = 0) -> dict:
    key_of = jax.random.split(jax.random.key(seed), 6)
    in_flight = noise(key_of[0], (NZ, 4, NY, NX), 1.0, 6.0, ((0, 16), (2, 2)), jnp.float32)
    entering = noise(key_of[1], (TURNS - 1, 4, NY, NX), 1.0, 6.0, ((2, 2),), jnp.float32)
    classes = plant(jax.random.randint(key_of[2], (NZ, NY, NX), 0, CLASSES), jax.random.fold_in(key_of[2], 1), 0, CLASSES - 1).astype(jnp.int32)
    freq_phase = jnp.clip(jnp.exp(jax.random.uniform(key_of[3], (FREQS,), jnp.float32, math.log(4.0), math.log(8.5))), 4.0, 8.5)
    class_slowness = jnp.clip(jnp.exp(jax.random.uniform(key_of[4], (CLASSES,), jnp.float32, math.log(0.8), math.log(1.4))), 0.8, 1.4)
    return dict(in_flight=in_flight, entering=entering, classes=classes, freq_phase=freq_phase, class_slowness=class_slowness)


hale_weight = 0.0255
centre_weight = -0.5 + hale_weight
edge_weight = 0.25 - 0.5 * hale_weight
corner_weight = 0.125 + 0.25 * hale_weight
miller_start = 32


def stencil(padded):
    centre = padded[:, 1:-1, 1:-1]
    edge_sum = padded[:, :-2, 1:-1] + padded[:, 2:, 1:-1] + padded[:, 1:-1, :-2] + padded[:, 1:-1, 2:]
    corners = padded[:, :-2, :-2] + padded[:, :-2, 2:] + padded[:, 2:, :-2] + padded[:, 2:, 2:]
    return centre_weight * centre + edge_weight * edge_sum + corner_weight * corners


def bessel_table(phases):
    values = [None] * (miller_start + 1)
    upper = jnp.zeros_like(phases)
    current = jnp.ones_like(phases)
    values[miller_start] = current
    for k in range(miller_start, 0, -1):
        lower = (2.0 * k / phases) * current - upper
        values[k - 1] = lower
        upper, current = current, lower
    evens = values[2]
    for k in range(4, miller_start + 1, 2):
        evens = evens + values[k]
    scale = values[0] + 2.0 * evens
    result = []
    for k in range(TERMS):
        ratio = values[k] / scale
        result.append(ratio if k == 0 else 2.0 * ratio)
    return jnp.stack(result)


def rotate(coefficient, k, fields):
    cycle_real = jnp.array([1.0, 0.0, -1.0, 0.0], fields.dtype)
    cycle_imag = jnp.array([0.0, 1.0, 0.0, -1.0], fields.dtype)
    real_part = coefficient * cycle_real[k % 4]
    imag_part = coefficient * cycle_imag[k % 4]
    return jnp.stack([real_part * fields[0] - imag_part * fields[1],
                      real_part * fields[1] + imag_part * fields[0],
                      real_part * fields[2] + imag_part * fields[3],
                      real_part * fields[3] - imag_part * fields[2]])


def correlate(extended, strip_rows):
    half_offset = OFFSETS // 2
    products = []
    for o in range(OFFSETS):
        lag = o - half_offset
        source = extended[:, half_offset - lag:half_offset - lag + strip_rows]
        receiver = extended[:, half_offset + lag:half_offset + lag + strip_rows]
        products.append(source[0] * receiver[2] + source[1] * receiver[3])
    return jnp.stack(products)


def extrapolate(fields, bessel):
    def apply_whole(current):
        return stencil(jnp.pad(current, ((0, 0), (1, 1), (1, 1))))

    first_term = apply_whole(fields)
    summed = rotate(bessel[0], 0, fields) + rotate(bessel[1], 1, first_term)

    def advance(k, carried):
        previous, current, running = carried
        following = 2.0 * apply_whole(current) - previous
        coefficient = lax.dynamic_index_in_dim(bessel, k + 1, 0, False)
        return (current, following, running + rotate(coefficient, k + 1, following))

    return lax.fori_loop(1, TERMS - 1, advance, (fields, first_term, summed))[2]


def reference(in_flight, entering, classes, freq_phase, class_slowness):
    wavefield = in_flight
    images = jnp.zeros((NZ, OFFSETS, NY, NX), in_flight.dtype)
    slab_ids = jnp.arange(NZ, dtype=jnp.int32)
    half_offset = OFFSETS // 2
    advanced = in_flight
    for turn_index in range(TURNS):
        freq_ids = (turn_index + NZ - 1 - slab_ids).astype(jnp.int32)

        def per_slab(inputs):
            fields, slab_classes, freq_index = inputs
            coeff_table = bessel_table(freq_phase[freq_index] * class_slowness)
            bessel = coeff_table[:, slab_classes]
            moved_on = extrapolate(fields, bessel)
            extended = jnp.pad(moved_on, ((0, 0), (half_offset, half_offset), (0, 0)))
            return moved_on, correlate(extended, NY)

        advanced, partial_value = lax.map(per_slab, (wavefield, classes, freq_ids))
        images = images + partial_value
        if turn_index + 1 < TURNS:
            wavefield = jnp.concatenate([entering[turn_index][None], advanced[:-1]], 0)
    return images, advanced
```

```python
import functools

import jax
import jax.numpy as jnp
from jax import lax
from jax.experimental import pallas as pl
from jax.experimental.pallas import tpu as pltpu
from jax.sharding import PartitionSpec as P

TERMS = 16
OFFSETS = 8
TURNS = 3
LANES = 128
SUBLANES = 8
BLOCKS = 4
MARGIN = OFFSETS // 2
VMEM_BYTES = 4 << 20

hale_weight = 0.0255
edge_weight = 0.25 - 0.5 * hale_weight
corner_weight = 0.125 + 0.25 * hale_weight
miller_start = 32

VMEM = pl.BlockSpec(memory_space=pltpu.VMEM)
SMEM = pl.BlockSpec(memory_space=pltpu.SMEM)
ANY = pl.BlockSpec(memory_space=pl.ANY)


def call(kernel, outs, in_specs, scratch, args, flops=0):
    moved = 4 * sum(int(a.size) for a in (*args, *outs))
    return pl.pallas_call(
        kernel,
        out_shape=outs,
        in_specs=in_specs,
        out_specs=[VMEM] * len(outs),
        scratch_shapes=scratch,
        compiler_params=pltpu.CompilerParams(vmem_limit_bytes=VMEM_BYTES),
        cost_estimate=pl.CostEstimate(flops=flops, bytes_accessed=moved, transcendentals=0),
    )(*args)


def f32(*shape):
    return jax.ShapeDtypeStruct(shape, jnp.float32)


def table_kernel(phase_ref, slow_ref, out_ref, z_ref):
    first = lax.axis_size("depth") - 1 - lax.axis_index("depth")
    classes = slow_ref.shape[1]
    z_ref[...] = jnp.full(z_ref.shape, 6.0, jnp.float32)
    for turn in range(TURNS):
        z_ref[turn : turn + 1, 0:classes] = slow_ref[...] * phase_ref[first + turn]
    phases = z_ref[...]
    values = [None] * (miller_start + 1)
    upper = jnp.zeros_like(phases)
    current = jnp.ones_like(phases)
    values[miller_start] = current
    inverse = 1.0 / phases
    for k in range(miller_start, 0, -1):
        lower = (2.0 * k * inverse) * current - upper
        values[k - 1] = lower
        upper, current = current, lower
    evens = values[2]
    for k in range(4, miller_start + 1, 2):
        evens = evens + values[k]
    scale = 1.0 / (values[0] + 2.0 * evens)
    for k in range(TERMS):
        factor = (1.0 if k == 0 else 2.0) * (1.0 if k % 4 < 2 else -1.0)
        ratio = values[k] * scale * factor
        for turn in range(TURNS):
            out_ref[turn, k] = jnp.broadcast_to(ratio[turn : turn + 1, :], (SUBLANES, LANES))


def advance(a, b, even, odd, classes, table, turn, sigma, valid_rows, emit):
    length, tiles = a.shape[0], a.shape[1]
    tile = (SUBLANES, LANES)
    lane = lax.broadcasted_iota(jnp.int32, tile, 1)
    sublane = lax.broadcasted_iota(jnp.int32, tile, 0)
    block = sublane % BLOCKS
    at_left, at_right = lane == 0, lane == LANES - 1
    zero = jnp.zeros(tile, jnp.float32)

    def doubled(source, i, rows):
        above, middle, below = rows
        spread, straight = [], []
        for h in range(tiles):
            vertical = above[h] + below[h]
            edge = (2.0 * edge_weight) * middle[h]
            spread.append((2.0 * corner_weight) * vertical + edge)
            straight.append((2.0 * edge_weight) * vertical - (edge + edge))
        from_left = [pltpu.roll(q, 1, 1) for q in spread]
        from_right = [pltpu.roll(q, LANES - 1, 1) for q in spread]
        result = []
        for h in range(tiles):
            left = jnp.where(at_left, from_left[h - 1] if h else zero, from_left[h])
            right = jnp.where(at_right, from_right[h + 1] if h + 1 < tiles else zero, from_right[h])
            result.append((left + right) + straight[h])
        return result

    def sweep(source, target, k, total, first):
        wrap_above = [
            jnp.where(block == 0, zero, pltpu.roll(source[length - 1, h], 1, 0)) for h in range(tiles)
        ]
        wrap_below = [
            jnp.where(block == BLOCKS - 1, zero, pltpu.roll(source[0, h], SUBLANES - 1, 0))
            for h in range(tiles)
        ]
        row = table[turn, k]
        above, middle = wrap_above, [source[0, h] for h in range(tiles)]
        for i in range(length):
            below = [source[i + 1, h] for h in range(tiles)] if i + 1 < length else wrap_below
            result = doubled(source, i, (above, middle, below))
            if valid_rows is not None:
                at = block * length + i
                inside = (at >= valid_rows[0]) & (at < valid_rows[1])
            for h in range(tiles):
                value = 0.5 * result[h] if first else result[h] - target[i, h]
                if valid_rows is not None:
                    value = jnp.where(inside, value, zero)
                target[i, h] = value
                coefficient = jnp.take_along_axis(row, classes[i, h], axis=1, mode="promise_in_bounds")
                term = coefficient * value
                if first:
                    total[i, h] = term
                    start = jnp.take_along_axis(
                        table[turn, 0], classes[i, h], axis=1, mode="promise_in_bounds"
                    )
                    even[i, h] = start * source[i, h]
                else:
                    total[i, h] = total[i, h] + term
            above, middle = middle, below

    sweep(a, b, 1, odd, True)

    def pair(n, carry):
        sweep(b, a, 2 * n, even, False)
        sweep(a, b, 2 * n + 1, odd, False)
        return carry

    lax.fori_loop(1, TERMS // 2, pair, 0)
    turned = jnp.where(sublane < BLOCKS, -sigma, sigma)
    for i in range(length):
        for h in range(tiles):
            emit(i, h, even[i, h] + turned * pltpu.roll(odd[i, h], BLOCKS, 0))


def sign_of(side):
    return jnp.where(side == 0, 1.0, -1.0).astype(jnp.float32)


def gather_blocks(natural, target, count):
    length = target.shape[0]
    for h in range(target.shape[1]):
        for i in range(length):
            target[i, h] = natural[h, pl.ds(PAD + i, count, stride=length), :]


PAD = 8


def windows(natural, length, strip_rows, side, own_ref, send_ref):
    rows = BLOCKS * length
    tall = strip_rows + 2 * MARGIN
    at = lax.broadcasted_iota(jnp.int32, (tall, LANES), 0)
    for ref, strip in ((own_ref, side), (send_ref, 1 - side)):
        begin = strip * strip_rows - MARGIN
        inside = (at + begin >= 0) & (at + begin < rows)
        for component in range(2):
            for h in range(natural.shape[0]):
                found = natural[h, pl.ds(PAD + component * rows + begin, tall), :]
                ref[component, h] = jnp.where(inside, found, 0.0)


def place(natural, source, component, rows, row, count):
    for h in range(natural.shape[0]):
        natural[h, pl.ds(pl.multiple_of(PAD + component * rows + row, 8), count), :] = source[
            :, h * LANES : (h + 1) * LANES
        ]


def split_kernel(in_ref, class_ref, own_ref, send_ref, whole, whole_classes, sem):
    side = lax.axis_index("lat")
    fields = pltpu.make_async_copy(in_ref.at[0], whole, sem.at[0])
    cells = pltpu.make_async_copy(class_ref.at[0], whole_classes, sem.at[1])
    fields.start()
    cells.start()
    cells.wait()
    as_float = whole_classes[...].astype(jnp.float32)
    own_ref[2] = as_float
    send_ref[2] = as_float
    fields.wait()
    for component in range(2):
        own_ref[component] = whole[side * 2 + component]
        send_ref[component] = whole[(1 - side) * 2 + component]


def first_kernel(own_ref, got_ref, table_ref, hand_ref, blocks_ref, mine_ref, send_ref, a, b, even, odd, natural):
    side = lax.axis_index("lat")
    strip_rows = own_ref.shape[1]
    rows = 2 * strip_rows
    length = a.shape[0]
    for component in range(2):
        place(natural, own_ref[2], component, rows, side * strip_rows, strip_rows)
        place(natural, got_ref[2], component, rows, (1 - side) * strip_rows, strip_rows)
    gather_blocks(natural, a, SUBLANES)
    for i in range(length):
        for h in range(a.shape[1]):
            blocks_ref[i, h] = a[i, h].astype(jnp.int32)
    for component in range(2):
        place(natural, own_ref[component], component, rows, side * strip_rows, strip_rows)
        place(natural, got_ref[component], component, rows, (1 - side) * strip_rows, strip_rows)
    gather_blocks(natural, a, SUBLANES)

    def emit(i, h, value):
        hand_ref[i, h] = value
        natural[h, pl.ds(PAD + i, SUBLANES, stride=length), :] = value

    advance(a, b, even, odd, blocks_ref, table_ref, 0, sign_of(side), None, emit)
    windows(natural, length, strip_rows, side, mine_ref, send_ref)


def next_kernel(turn, last, got_ref, enter_ref, enter_got_ref, blocks_ref, table_ref, *rest):
    if last:
        mine_ref, send_ref, a, b, even, odd, natural, strips, sem = rest
        hand_ref = None
    else:
        hand_ref, mine_ref, send_ref, a, b, even, odd, natural, strips, sem = rest
    side = lax.axis_index("lat")
    top = lax.axis_index("depth") == 0
    strip_rows = strips.shape[2]
    rows = 2 * strip_rows
    length = a.shape[0]

    @pl.when(top)
    def _():
        copies = []
        for j, ref in enumerate((enter_ref, enter_got_ref)):
            copies.append(
                pltpu.make_async_copy(ref.at[turn - 1, pl.ds(2 * side, 2)], strips.at[j], sem.at[j])
            )
        for copy in copies:
            copy.start()
        for copy in copies:
            copy.wait()
        for component in range(2):
            place(natural, strips[0, component], component, rows, side * strip_rows, strip_rows)
            place(natural, strips[1, component], component, rows, (1 - side) * strip_rows, strip_rows)
        gather_blocks(natural, a, SUBLANES)

    @pl.when(jnp.logical_not(top))
    def _():
        a[...] = got_ref[...]

    def emit(i, h, value):
        if not last:
            hand_ref[i, h] = value
        natural[h, pl.ds(PAD + i, SUBLANES, stride=length), :] = value

    advance(a, b, even, odd, blocks_ref, table_ref, turn, sign_of(side), None, emit)
    windows(natural, length, strip_rows, side, mine_ref, send_ref)


def image_kernel(*refs):
    pairs = [(refs[2 * t], refs[2 * t + 1]) for t in range(TURNS)]
    images_ref, wave_ref, source, receiver = refs[2 * TURNS :]
    side = lax.axis_index("lat")
    strip_rows = wave_ref.shape[2]
    tiles = source.shape[2]

    @pl.when(side == 0)
    def _():
        for t, (mine, got) in enumerate(pairs):
            source[t] = mine[...]
            receiver[t] = got[...]

    @pl.when(side == 1)
    def _():
        for t, (mine, got) in enumerate(pairs):
            source[t] = got[...]
            receiver[t] = mine[...]

    for h in range(tiles):
        at = slice(h * LANES, (h + 1) * LANES)
        for o in range(OFFSETS):
            lag = o - MARGIN
            total = None
            for t in range(TURNS):
                for component in range(2):
                    product = (
                        source[t, component, h, MARGIN - lag : MARGIN - lag + strip_rows, :]
                        * receiver[t, component, h, MARGIN + lag : MARGIN + lag + strip_rows, :]
                    )
                    total = product if total is None else total + product
            images_ref[0, o, :, at] = total
        for component in range(2):
            rows = slice(MARGIN, MARGIN + strip_rows)
            wave_ref[0, component, :, at] = source[TURNS - 1, component, h, rows, :]
            wave_ref[0, 2 + component, :, at] = receiver[TURNS - 1, component, h, rows, :]


def field_scratch(length, tiles):
    return [pltpu.VMEM((length, tiles, SUBLANES, LANES), jnp.float32)] * 4


def coefficients(freq_phase, class_slowness):
    (table,) = call(
        table_kernel,
        [f32(TURNS, TERMS, SUBLANES, LANES)],
        [SMEM, VMEM],
        [pltpu.VMEM((SUBLANES, LANES), jnp.float32)],
        (freq_phase, class_slowness.reshape(1, -1)),
    )
    return table


def paired(in_flight, entering, classes, freq_phase, class_slowness):
    depth = lax.axis_size("depth")
    _, _, strip_rows, width = in_flight.shape
    tiles = width // LANES
    length = 2 * strip_rows // BLOCKS
    swap = [(0, 1), (1, 0)]
    shift = [(i, i + 1) for i in range(depth - 1)]
    blocks = f32(length, tiles, SUBLANES, LANES)
    window = f32(2, tiles, strip_rows + 2 * MARGIN, LANES)
    natural = pltpu.VMEM((tiles, 2 * BLOCKS * length + 2 * PAD, LANES), jnp.float32)
    strips = f32(3, strip_rows, width)
    flops = 20 * TERMS * 2 * BLOCKS * length * width

    own, send = call(
        split_kernel,
        [strips, strips],
        [ANY, ANY],
        [
            pltpu.VMEM((4, strip_rows, width), jnp.float32),
            pltpu.VMEM((strip_rows, width), jnp.int32),
            pltpu.SemaphoreType.DMA((2,)),
        ],
        (in_flight, classes),
    )
    got = lax.ppermute(send, "lat", swap)
    enter_got = lax.ppermute(entering, ("depth", "lat"), swap)
    table = coefficients(freq_phase, class_slowness)
    hand, cells, mine, send = call(
        first_kernel,
        [blocks, jax.ShapeDtypeStruct(blocks.shape, jnp.int32), window, window],
        [VMEM] * 3,
        field_scratch(length, tiles) + [natural],
        (own, got, table),
        flops,
    )
    pairs = []
    for turn in range(1, TURNS):
        handed = lax.ppermute(hand, "depth", shift)
        pairs += [mine, lax.ppermute(send, "lat", swap)]
        last = turn == TURNS - 1
        outs = call(
            functools.partial(next_kernel, turn, last),
            ([] if last else [blocks]) + [window, window],
            [VMEM, ANY, ANY, VMEM, VMEM],
            field_scratch(length, tiles)
            + [natural, pltpu.VMEM((2, 2, strip_rows, width), jnp.float32), pltpu.SemaphoreType.DMA((2,))],
            (handed, entering, enter_got, cells, table),
            flops,
        )
        if last:
            mine, send = outs
        else:
            hand, mine, send = outs
    pairs += [mine, lax.ppermute(send, "lat", swap)]
    return tuple(
        call(
            image_kernel,
            [f32(1, OFFSETS, strip_rows, width), f32(1, 4, strip_rows, width)],
            [VMEM] * len(pairs),
            [pltpu.VMEM((TURNS, *window.shape), jnp.float32)] * 2,
            pairs,
        )
    )


def inside_kernel(turn, limits_ref, field_ref, blocks_ref, table_ref, out_ref, a, b, even, odd):
    a[...] = field_ref[...]

    def emit(i, h, value):
        out_ref[i, h] = value

    side = lax.axis_index("lat") % 2
    valid = (limits_ref[0], limits_ref[1])
    advance(a, b, even, odd, blocks_ref, table_ref, turn, sign_of(side), valid, emit)


def grouped(in_flight, entering, classes, freq_phase, class_slowness):
    depth, strips = lax.axis_size("depth"), lax.axis_size("lat")
    strip = lax.axis_index("lat")
    side, group = strip % 2, strip // 2
    _, _, strip_rows, width = in_flight.shape
    tiles = width // LANES
    core = 2 * strip_rows
    halo = TERMS - 1 + MARGIN
    while (core + 2 * halo) % BLOCKS:
        halo += 1
    rows = core + 2 * halo
    length = rows // BLOCKS
    swap = [(i, i ^ 1) for i in range(strips)]
    shift = [(i, i + 1) for i in range(depth - 1)]
    blocks = f32(length, tiles, SUBLANES, LANES)

    def both_strips(mine, sent):
        got = lax.ppermute(sent, "lat", swap)
        return jnp.where(
            side == 0, jnp.concatenate([mine, got], 1), jnp.concatenate([got, mine], 1)
        )

    def own_components(fields):
        return both_strips(
            lax.dynamic_slice_in_dim(fields, 2 * side, 2, 0),
            lax.dynamic_slice_in_dim(fields, 2 * (1 - side), 2, 0),
        )

    def with_halo(cells):
        above = lax.ppermute(cells[:, core - halo :], "lat", [(i, i + 2) for i in range(strips - 2)])
        below = lax.ppermute(cells[:, :halo], "lat", [(i + 2, i) for i in range(strips - 2)])
        return jnp.concatenate([above, cells, below], 1)

    def to_blocks(cells):
        split = cells.reshape(2, BLOCKS, length, tiles, LANES)
        return split.transpose(2, 3, 0, 1, 4).reshape(blocks.shape)

    def to_rows(cells):
        split = cells.reshape(length, tiles, 2, BLOCKS, LANES)
        return split.transpose(2, 3, 0, 1, 4).reshape(2, rows, width)

    def window(cells, which):
        begin = halo - MARGIN + which * strip_rows
        return lax.dynamic_slice_in_dim(cells, begin, strip_rows + 2 * MARGIN, 1)

    cells = with_halo(both_strips(classes, classes))
    cells = to_blocks(jnp.concatenate([cells, cells], 0))
    table = coefficients(freq_phase, class_slowness)
    before = group * core - halo
    limits = jnp.stack([jnp.maximum(-before, 0), jnp.minimum(strips * strip_rows - before, rows)])
    field = own_components(in_flight[0])
    images = jnp.zeros((OFFSETS, strip_rows, width), jnp.float32)
    for turn in range(TURNS):
        (advanced,) = call(
            functools.partial(inside_kernel, turn),
            [blocks],
            [SMEM, VMEM, VMEM, VMEM],
            field_scratch(length, tiles),
            (limits.astype(jnp.int32), to_blocks(with_halo(field)), cells, table),
        )
        advanced = to_rows(advanced)
        mine = window(advanced, side)
        got = lax.ppermute(window(advanced, 1 - side), "lat", swap)
        source, receiver = jnp.where(side == 0, mine, got), jnp.where(side == 0, got, mine)
        products = []
        for o in range(OFFSETS):
            lag = o - MARGIN
            first = source[:, MARGIN - lag : MARGIN - lag + strip_rows]
            second = receiver[:, MARGIN + lag : MARGIN + lag + strip_rows]
            products.append(first[0] * second[0] + first[1] * second[1])
        images = images + jnp.stack(products)
        if turn + 1 < TURNS:
            handed = lax.ppermute(advanced[:, halo : halo + core], "depth", shift)
            entered = own_components(entering[turn])
            field = jnp.where(lax.axis_index("depth") == 0, entered, handed)
    own = slice(MARGIN, MARGIN + strip_rows)
    return images[None], jnp.concatenate([source[:, own], receiver[:, own]], 0)[None]


def solution(mesh):
    in_specs = (
        P("depth", None, "lat", None),
        P(None, None, "lat", None),
        P("depth", "lat", None),
        P(),
        P(),
    )
    out_specs = (P("depth", None, "lat", None), P("depth", None, "lat", None))
    local = paired if mesh.shape["lat"] == 2 else grouped
    return jax.shard_map(local, mesh=mesh, in_specs=in_specs, out_specs=out_specs, check_vma=False)
```

```python
import functools

import jax
import jax.numpy as jnp
from jax import lax
from jax.experimental import pallas as pl
from jax.experimental.pallas import tpu as pltpu
from jax.sharding import PartitionSpec as P

TERMS = 16
OFFSETS = 8
TURNS = 3
LANES = 128
SUBLANES = 8
PLANE = 4
BLOCKS = 8
MARGIN = OFFSETS // 2
VMEM_BYTES = 4 << 20

hale_weight = 0.0255
edge_weight = 0.25 - 0.5 * hale_weight
corner_weight = 0.125 + 0.25 * hale_weight
miller_start = 32

VMEM = pl.BlockSpec(memory_space=pltpu.VMEM)
SMEM = pl.BlockSpec(memory_space=pltpu.SMEM)
HBM = pl.BlockSpec(memory_space=pltpu.HBM)
ANY = pl.BlockSpec(memory_space=pl.ANY)


def call(kernel, outs, in_specs, scratch, args, flops=0):
    moved = 4 * sum(int(a.size) for a in (*args, *outs))
    return pl.pallas_call(
        kernel,
        out_shape=outs,
        in_specs=in_specs,
        out_specs=[VMEM] * len(outs),
        scratch_shapes=scratch,
        compiler_params=pltpu.CompilerParams(vmem_limit_bytes=VMEM_BYTES),
        cost_estimate=pl.CostEstimate(flops=flops, bytes_accessed=moved, transcendentals=0),
    )(*args)


def in_hbm(*arrays):
    return tuple(pltpu.with_memory_space_constraint(x, pltpu.HBM) for x in arrays)


def f32(*shape):
    return jax.ShapeDtypeStruct(shape, jnp.float32)


def table_kernel(phase_hbm, slow_hbm, out_ref, z_ref, phase_ref, slow_ref, sem):
    copies = [
        pltpu.make_async_copy(phase_hbm, phase_ref, sem.at[0]),
        pltpu.make_async_copy(slow_hbm, slow_ref, sem.at[1]),
    ]
    for copy in copies:
        copy.start()
    for copy in copies:
        copy.wait()
    first = lax.axis_size("depth") - 1 - lax.axis_index("depth")
    classes = slow_ref.shape[1]
    z_ref[...] = jnp.full(z_ref.shape, 6.0, jnp.float32)
    for turn in range(TURNS):
        z_ref[turn : turn + 1, 0:classes] = slow_ref[...] * phase_ref[first + turn]
    phases = z_ref[...]
    values = [None] * (miller_start + 1)
    upper = jnp.zeros_like(phases)
    current = jnp.ones_like(phases)
    values[miller_start] = current
    inverse = 1.0 / phases
    for k in range(miller_start, 0, -1):
        lower = (2.0 * k * inverse) * current - upper
        values[k - 1] = lower
        upper, current = current, lower
    evens = values[2]
    for k in range(4, miller_start + 1, 2):
        evens = evens + values[k]
    scale = 1.0 / (values[0] + 2.0 * evens)
    for k in range(TERMS):
        factor = (1.0 if k == 0 else 2.0) * (1.0 if k % 4 < 2 else -1.0)
        ratio = values[k] * scale * factor
        for turn in range(TURNS):
            out_ref[turn, k] = jnp.broadcast_to(ratio[turn : turn + 1, :], (SUBLANES, LANES))


def pick(row, classes):
    dimensions = lax.GatherDimensionNumbers(
        offset_dims=(),
        collapsed_slice_dims=(1,),
        start_index_map=(1,),
        operand_batching_dims=(0,),
        start_indices_batching_dims=(0,),
    )
    return lax.gather(
        row, classes[..., None], dimensions, (1, 1), mode=lax.GatherScatterMode.PROMISE_IN_BOUNDS
    )


def advance(a, b, total, classes, table, turn, sigma, valid_rows, emit):
    length, tiles = a.shape[1], a.shape[2]
    tile = (SUBLANES, LANES)
    lane = lax.broadcasted_iota(jnp.int32, tile, 1)
    block = lax.broadcasted_iota(jnp.int32, tile, 0)
    at_left, at_right = lane == 0, lane == LANES - 1
    zero = jnp.zeros(tile, jnp.float32)

    def doubled(above, middle, below):
        spread, straight = [], []
        for h in range(tiles):
            vertical = above[h] + below[h]
            edge = (2.0 * edge_weight) * middle[h]
            spread.append((2.0 * corner_weight) * vertical + edge)
            straight.append((2.0 * edge_weight) * vertical - (edge + edge))
        from_left = [pltpu.roll(q, 1, 1) for q in spread]
        from_right = [pltpu.roll(q, LANES - 1, 1) for q in spread]
        result = []
        for h in range(tiles):
            left = jnp.where(at_left, from_left[h - 1] if h else zero, from_left[h])
            right = jnp.where(at_right, from_right[h + 1] if h + 1 < tiles else zero, from_right[h])
            result.append((left + right) + straight[h])
        return result

    def sweep(source, target, k, odd, first):
        def row_of(c, i):
            if i < 0:
                return [
                    jnp.where(block == 0, zero, pltpu.roll(source[c, length - 1, h], 1, 0))
                    for h in range(tiles)
                ]
            if i == length:
                return [
                    jnp.where(block == BLOCKS - 1, zero, pltpu.roll(source[c, 0, h], SUBLANES - 1, 0))
                    for h in range(tiles)
                ]
            return [source[c, i, h] for h in range(tiles)]

        row = table[turn, k]
        if odd:
            row = row * sigma
        near = [(row_of(c, -1), row_of(c, 0)) for c in range(2)]
        for i in range(length):
            if valid_rows is not None:
                at = block * length + i
                inside = (at >= valid_rows[0]) & (at < valid_rows[1])
            values = []
            for c in range(2):
                above, middle = near[c]
                below = row_of(c, i + 1)
                near[c] = (middle, below)
                result = doubled(above, middle, below)
                for h in range(tiles):
                    value = 0.5 * result[h] if first else result[h] - target[c, i, h]
                    if valid_rows is not None:
                        value = jnp.where(inside, value, zero)
                    target[c, i, h] = value
                    result[h] = value
                values.append(result)
            for h in range(tiles):
                at_class = classes[i, h]
                coefficient = pick(row, at_class)
                if first:
                    start = pick(table[turn, 0], at_class)
                    sums = [start * source[c, i, h] for c in range(2)]
                else:
                    sums = [total[c, i, h] for c in range(2)]
                if odd:
                    total[0, i, h] = sums[0] - coefficient * values[1][h]
                    total[1, i, h] = sums[1] + coefficient * values[0][h]
                else:
                    total[0, i, h] = sums[0] + coefficient * values[0][h]
                    total[1, i, h] = sums[1] + coefficient * values[1][h]

    sweep(a, b, 1, True, True)

    def pair(n, carry):
        sweep(b, a, 2 * n, False, False)
        sweep(a, b, 2 * n + 1, True, False)
        return carry

    lax.fori_loop(1, TERMS // 2, pair, 0)
    for c in range(2):
        for i in range(length):
            for h in range(tiles):
                emit(c, i, h, total[c, i, h])


def sign_of(side):
    return jnp.where(side == 0, 1.0, -1.0).astype(jnp.float32)


def block_of(natural, c, i, h, length):
    return natural[h, pl.ds(PAD + c * BLOCKS * length + i, BLOCKS, stride=length), :]


def gather_blocks(natural, target):
    length = target.shape[1]
    for c in range(2):
        for i in range(length):
            for h in range(target.shape[2]):
                target[c, i, h] = block_of(natural, c, i, h, length)


PAD = 8


def windows(natural, length, strip_rows, side, own_ref, send_ref):
    rows = BLOCKS * length
    tall = strip_rows + 2 * MARGIN
    at = lax.broadcasted_iota(jnp.int32, (tall, LANES), 0)
    for ref, strip in ((own_ref, side), (send_ref, 1 - side)):
        begin = strip * strip_rows - MARGIN
        inside = (at + begin >= 0) & (at + begin < rows)
        for component in range(2):
            for h in range(natural.shape[0]):
                found = natural[h, pl.ds(PAD + component * rows + begin, tall), :]
                ref[component, h] = jnp.where(inside, found, 0.0)


def place(natural, source, component, rows, row, count):
    for h in range(natural.shape[0]):
        natural[h, pl.ds(pl.multiple_of(PAD + component * rows + row, 8), count), :] = source[
            :, h * LANES : (h + 1) * LANES
        ]


def split_kernel(in_ref, class_ref, own_ref, send_ref, whole, whole_classes, sem):
    side = lax.axis_index("lat")
    fields = pltpu.make_async_copy(in_ref.at[0], whole, sem.at[0])
    cells = pltpu.make_async_copy(class_ref.at[0], whole_classes, sem.at[1])
    fields.start()
    cells.start()
    cells.wait()
    as_float = whole_classes[...].astype(jnp.float32)
    own_ref[2] = as_float
    send_ref[2] = as_float
    fields.wait()
    for component in range(2):
        own_ref[component] = whole[side * 2 + component]
        send_ref[component] = whole[(1 - side) * 2 + component]


def pack(strips, target):
    for component in range(2):
        for j in range(strips.shape[1] // SUBLANES):
            for h in range(target.shape[2]):
                at = (component, slice(j * SUBLANES, (j + 1) * SUBLANES), slice(h * LANES, (h + 1) * LANES))
                target[component, j, h] = strips[at]


def unpack(source, natural, component, rows, row, count):
    for h in range(natural.shape[0]):
        for j in range(count // SUBLANES):
            at = pl.multiple_of(PAD + component * rows + row + j * SUBLANES, 8)
            natural[h, pl.ds(at, SUBLANES), :] = source[component, j, h]


def turn_of(turn, a, b, total, natural, blocks_ref, table_ref, enter_ref, strip, sem, outs):
    side = lax.axis_index("lat")
    length = a.shape[1]
    rows = BLOCKS * length
    mine_ref, send_ref = outs[-2:]
    last = len(outs) == 2
    top = lax.axis_index("depth") == 0
    if not last:
        hand_ref, cross_ref = outs[:2]
        fetch = pltpu.make_async_copy(enter_ref.at[turn, pl.ds(2 * (1 - side), 2)], strip, sem)
        fetch.start()

    def emit(c, i, h, value):
        if not last:
            hand_ref[c, i, h] = value
            cross_ref[c, i, h] = value
        natural[h, pl.ds(PAD + c * rows + i, BLOCKS, stride=length), :] = value

    advance(a, b, total, blocks_ref, table_ref, turn, sign_of(side), None, emit)
    windows(natural, length, rows // 2, side, mine_ref, send_ref)
    if not last:
        fetch.wait()

        @pl.when(top)
        def _():
            pack(strip, cross_ref)


def first_kernel(own_ref, got_ref, table_ref, enter_ref, *rest):
    hand_ref, cross_ref, blocks_ref, mine_ref, send_ref, a, b, total, natural, strip, sem = rest
    side = lax.axis_index("lat")
    strip_rows = own_ref.shape[1]
    rows = 2 * strip_rows
    length = a.shape[1]
    place(natural, own_ref[2], 0, rows, side * strip_rows, strip_rows)
    place(natural, got_ref[2], 0, rows, (1 - side) * strip_rows, strip_rows)
    for i in range(length):
        for h in range(a.shape[2]):
            blocks_ref[i, h] = block_of(natural, 0, i, h, length).astype(jnp.int32)
    for component in range(2):
        place(natural, own_ref[component], component, rows, side * strip_rows, strip_rows)
        place(natural, got_ref[component], component, rows, (1 - side) * strip_rows, strip_rows)
    gather_blocks(natural, a)
    outs = (hand_ref, cross_ref, mine_ref, send_ref)
    turn_of(0, a, b, total, natural, blocks_ref, table_ref, enter_ref, strip, sem.at[0], outs)


def next_kernel(turn, plane, got_ref, crossed_ref, blocks_ref, table_ref, enter_ref, *rest):
    *outs, a, b, total, natural, strip, sem = rest
    side = lax.axis_index("lat")
    slab = lax.axis_index("depth")
    strip_rows = strip.shape[1]
    rows = 2 * strip_rows

    @pl.when(slab == 0)
    def _():
        fetch = pltpu.make_async_copy(enter_ref.at[turn - 1, pl.ds(2 * side, 2)], strip, sem.at[1])
        fetch.start()
        fetch.wait()
        for component in range(2):
            place(natural, strip[component], component, rows, side * strip_rows, strip_rows)
            unpack(crossed_ref, natural, component, rows, (1 - side) * strip_rows, strip_rows)
        gather_blocks(natural, a)

    @pl.when((slab > 0) & (slab % plane == 0))
    def _():
        a[...] = crossed_ref[...]

    @pl.when(slab % plane > 0)
    def _():
        a[...] = got_ref[...]

    turn_of(turn, a, b, total, natural, blocks_ref, table_ref, enter_ref, strip, sem.at[0], outs)


def image_kernel(*refs):
    pairs = [(refs[2 * t], refs[2 * t + 1]) for t in range(TURNS)]
    images_ref, wave_ref, source, receiver = refs[2 * TURNS :]
    side = lax.axis_index("lat")
    strip_rows = wave_ref.shape[2]
    tiles = source.shape[2]

    @pl.when(side == 0)
    def _():
        for t, (mine, got) in enumerate(pairs):
            source[t] = mine[...]
            receiver[t] = got[...]

    @pl.when(side == 1)
    def _():
        for t, (mine, got) in enumerate(pairs):
            source[t] = got[...]
            receiver[t] = mine[...]

    for h in range(tiles):
        at = slice(h * LANES, (h + 1) * LANES)
        for o in range(OFFSETS):
            lag = o - MARGIN
            total = None
            for t in range(TURNS):
                for component in range(2):
                    product = (
                        source[t, component, h, MARGIN - lag : MARGIN - lag + strip_rows, :]
                        * receiver[t, component, h, MARGIN + lag : MARGIN + lag + strip_rows, :]
                    )
                    total = product if total is None else total + product
            images_ref[0, o, :, at] = total
        for component in range(2):
            rows = slice(MARGIN, MARGIN + strip_rows)
            wave_ref[0, component, :, at] = source[TURNS - 1, component, h, rows, :]
            wave_ref[0, 2 + component, :, at] = receiver[TURNS - 1, component, h, rows, :]


def field_scratch(length, tiles):
    return [pltpu.VMEM((2, length, tiles, BLOCKS, LANES), jnp.float32)] * 3


def coefficients(freq_phase, class_slowness):
    (table,) = call(
        table_kernel,
        [f32(TURNS, TERMS, SUBLANES, LANES)],
        [HBM, HBM],
        [
            pltpu.VMEM((SUBLANES, LANES), jnp.float32),
            pltpu.SMEM(freq_phase.shape, jnp.float32),
            pltpu.VMEM((1, class_slowness.shape[0]), jnp.float32),
            pltpu.SemaphoreType.DMA((2,)),
        ],
        in_hbm(freq_phase, class_slowness.reshape(1, -1)),
    )
    return table


def paired(in_flight, entering, classes, freq_phase, class_slowness):
    depth = lax.axis_size("depth")
    _, _, strip_rows, width = in_flight.shape
    tiles = width // LANES
    length = 2 * strip_rows // BLOCKS
    swap = [(0, 1), (1, 0)]
    plane = PLANE if depth % PLANE == 0 else depth
    ring = [(i, i - i % plane + (i + 1) % plane) for i in range(depth)]
    across = {}
    for first in range(plane, depth, plane):
        across[first - 1], across[first] = first, first - 1
    cross = [
        (2 * d + c, 2 * across[d] + c if d in across else 2 * d + 1 - c)
        for d in range(depth)
        for c in range(2)
    ]
    blocks = f32(2, length, tiles, BLOCKS, LANES)
    window = f32(2, tiles, strip_rows + 2 * MARGIN, LANES)
    natural = pltpu.VMEM((tiles, 2 * BLOCKS * length + 2 * PAD, LANES), jnp.float32)
    scratch = field_scratch(length, tiles) + [
        natural,
        pltpu.VMEM((2, strip_rows, width), jnp.float32),
        pltpu.SemaphoreType.DMA((2,)),
    ]
    strips = f32(3, strip_rows, width)
    flops = 20 * TERMS * 4 * strip_rows * width

    own, send = call(
        split_kernel,
        [strips, strips],
        [HBM, HBM],
        [
            pltpu.VMEM((4, strip_rows, width), jnp.float32),
            pltpu.VMEM((strip_rows, width), jnp.int32),
            pltpu.SemaphoreType.DMA((2,)),
        ],
        in_hbm(in_flight, classes),
    )
    got = lax.ppermute(send, "lat", swap)
    freq_phase, _ = lax.optimization_barrier((freq_phase, own))
    table = coefficients(freq_phase, class_slowness)
    hand, over, cells, mine, send = call(
        first_kernel,
        [blocks, blocks, jax.ShapeDtypeStruct(blocks.shape[1:], jnp.int32), window, window],
        [VMEM, VMEM, VMEM, HBM],
        scratch,
        (own, got, table, entering),
        flops,
    )
    pairs = []
    for turn in range(1, TURNS):
        handed = lax.ppermute(hand, "depth", ring)
        crossed = lax.ppermute(over, ("depth", "lat"), cross)
        pairs += [mine, lax.ppermute(send, "lat", swap)]
        last = turn == TURNS - 1
        outs = call(
            functools.partial(next_kernel, turn, plane),
            ([] if last else [blocks, blocks]) + [window, window],
            [VMEM, VMEM, VMEM, VMEM, HBM],
            scratch,
            (handed, crossed, cells, table, entering),
            flops,
        )
        if last:
            mine, send = outs
        else:
            hand, over, mine, send = outs
    pairs += [mine, lax.ppermute(send, "lat", swap)]
    return tuple(
        call(
            image_kernel,
            [f32(1, OFFSETS, strip_rows, width), f32(1, 4, strip_rows, width)],
            [VMEM] * len(pairs),
            [pltpu.VMEM((TURNS, *window.shape), jnp.float32)] * 2,
            pairs,
        )
    )


def inside_kernel(turn, limits_ref, field_ref, blocks_ref, table_ref, out_ref, a, b, total):
    a[...] = field_ref[...]

    def emit(c, i, h, value):
        out_ref[c, i, h] = value

    side = lax.axis_index("lat") % 2
    valid = (limits_ref[0], limits_ref[1])
    advance(a, b, total, blocks_ref, table_ref, turn, sign_of(side), valid, emit)


def grouped(in_flight, entering, classes, freq_phase, class_slowness):
    depth, strips = lax.axis_size("depth"), lax.axis_size("lat")
    strip = lax.axis_index("lat")
    side, group = strip % 2, strip // 2
    _, _, strip_rows, width = in_flight.shape
    tiles = width // LANES
    core = 2 * strip_rows
    halo = TERMS - 1 + MARGIN
    while (core + 2 * halo) % BLOCKS:
        halo += 1
    rows = core + 2 * halo
    length = rows // BLOCKS
    swap = [(i, i ^ 1) for i in range(strips)]
    shift = [(i, i + 1) for i in range(depth - 1)]
    blocks = f32(2, length, tiles, BLOCKS, LANES)

    def both_strips(mine, sent):
        got = lax.ppermute(sent, "lat", swap)
        return jnp.where(
            side == 0, jnp.concatenate([mine, got], 1), jnp.concatenate([got, mine], 1)
        )

    def own_components(fields):
        return both_strips(
            lax.dynamic_slice_in_dim(fields, 2 * side, 2, 0),
            lax.dynamic_slice_in_dim(fields, 2 * (1 - side), 2, 0),
        )

    def with_halo(cells):
        above = lax.ppermute(cells[:, core - halo :], "lat", [(i, i + 2) for i in range(strips - 2)])
        below = lax.ppermute(cells[:, :halo], "lat", [(i + 2, i) for i in range(strips - 2)])
        return jnp.concatenate([above, cells, below], 1)

    def to_blocks(cells):
        split = cells.reshape(-1, BLOCKS, length, tiles, LANES)
        return split.transpose(0, 2, 3, 1, 4)

    def to_rows(cells):
        return cells.transpose(0, 3, 1, 2, 4).reshape(2, rows, width)

    def window(cells, which):
        begin = halo - MARGIN + which * strip_rows
        return lax.dynamic_slice_in_dim(cells, begin, strip_rows + 2 * MARGIN, 1)

    cells = to_blocks(with_halo(both_strips(classes, classes)))[0]
    table = coefficients(freq_phase, class_slowness)
    before = group * core - halo
    limits = jnp.stack([jnp.maximum(-before, 0), jnp.minimum(strips * strip_rows - before, rows)])
    field = own_components(in_flight[0])
    images = jnp.zeros((OFFSETS, strip_rows, width), jnp.float32)
    for turn in range(TURNS):
        (advanced,) = call(
            functools.partial(inside_kernel, turn),
            [blocks],
            [SMEM, VMEM, VMEM, VMEM],
            field_scratch(length, tiles),
            (limits.astype(jnp.int32), to_blocks(with_halo(field)), cells, table),
        )
        advanced = to_rows(advanced)
        mine = window(advanced, side)
        got = lax.ppermute(window(advanced, 1 - side), "lat", swap)
        source, receiver = jnp.where(side == 0, mine, got), jnp.where(side == 0, got, mine)
        products = []
        for o in range(OFFSETS):
            lag = o - MARGIN
            first = source[:, MARGIN - lag : MARGIN - lag + strip_rows]
            second = receiver[:, MARGIN + lag : MARGIN + lag + strip_rows]
            products.append(first[0] * second[0] + first[1] * second[1])
        images = images + jnp.stack(products)
        if turn + 1 < TURNS:
            handed = lax.ppermute(advanced[:, halo : halo + core], "depth", shift)
            entered = own_components(entering[turn])
            field = jnp.where(lax.axis_index("depth") == 0, entered, handed)
    own = slice(MARGIN, MARGIN + strip_rows)
    return images[None], jnp.concatenate([source[:, own], receiver[:, own]], 0)[None]


def solution(mesh):
    in_specs = (
        P("depth", None, "lat", None),
        P(None, None, "lat", None),
        P("depth", "lat", None),
        P(),
        P(),
    )
    out_specs = (P("depth", None, "lat", None), P("depth", None, "lat", None))
    local = paired if mesh.shape["lat"] == 2 else grouped
    return jax.shard_map(local, mesh=mesh, in_specs=in_specs, out_specs=out_specs, check_vma=False)
```

```python
import functools

import jax
import jax.numpy as jnp
from jax import lax
from jax.experimental import pallas as pl
from jax.experimental.pallas import tpu as pltpu
from jax.sharding import PartitionSpec as P

TERMS = 16
OFFSETS = 8
TURNS = 3
LANES = 128
SUBLANES = 8
PLANE = 4
BLOCKS = 8
MARGIN = OFFSETS // 2
VMEM_BYTES = 4 << 20

hale_weight = 0.0255
edge_weight = 0.25 - 0.5 * hale_weight
corner_weight = 0.125 + 0.25 * hale_weight
growth = 1.0 / (2.0 * edge_weight)
miller_start = 32

VMEM = pl.BlockSpec(memory_space=pltpu.VMEM)
SMEM = pl.BlockSpec(memory_space=pltpu.SMEM)
HBM = pl.BlockSpec(memory_space=pltpu.HBM)
ANY = pl.BlockSpec(memory_space=pl.ANY)


def call(kernel, outs, in_specs, scratch, args, flops=0, out_specs=None):
    moved = 4 * sum(int(a.size) for a in (*args, *outs))
    return pl.pallas_call(
        kernel,
        out_shape=outs,
        in_specs=in_specs,
        out_specs=out_specs or [VMEM] * len(outs),
        scratch_shapes=scratch,
        compiler_params=pltpu.CompilerParams(vmem_limit_bytes=VMEM_BYTES),
        cost_estimate=pl.CostEstimate(flops=flops, bytes_accessed=moved, transcendentals=0),
    )(*args)


def in_hbm(*arrays):
    return tuple(pltpu.with_memory_space_constraint(x, pltpu.HBM) for x in arrays)


def f32(*shape):
    return jax.ShapeDtypeStruct(shape, jnp.float32)


def table_kernel(phase_hbm, slow_hbm, out_ref, z_ref, phase_ref, slow_ref, sem):
    copies = [
        pltpu.make_async_copy(phase_hbm, phase_ref, sem.at[0]),
        pltpu.make_async_copy(slow_hbm, slow_ref, sem.at[1]),
    ]
    for copy in copies:
        copy.start()
    for copy in copies:
        copy.wait()
    first = lax.axis_size("depth") - 1 - lax.axis_index("depth")
    classes = slow_ref.shape[1]
    z_ref[...] = jnp.full(z_ref.shape, 6.0, jnp.float32)
    for turn in range(TURNS):
        z_ref[turn : turn + 1, 0:classes] = slow_ref[...] * phase_ref[first + turn]
    phases = z_ref[...]
    values = [None] * (miller_start + 1)
    upper = jnp.zeros_like(phases)
    current = jnp.ones_like(phases)
    values[miller_start] = current
    inverse = 1.0 / phases
    for k in range(miller_start, 0, -1):
        lower = (2.0 * k * inverse) * current - upper
        values[k - 1] = lower
        upper, current = current, lower
    evens = values[2]
    for k in range(4, miller_start + 1, 2):
        evens = evens + values[k]
    scale = 1.0 / (values[0] + 2.0 * evens)
    for k in range(TERMS):
        factor = (1.0 if k == 0 else 2.0) * (1.0 if k % 4 < 2 else -1.0) * growth**-k
        ratio = values[k] * scale * factor
        for turn in range(TURNS):
            out_ref[turn, k] = jnp.broadcast_to(ratio[turn : turn + 1, :], (SUBLANES, LANES))


def pick(row, classes):
    dimensions = lax.GatherDimensionNumbers(
        offset_dims=(),
        collapsed_slice_dims=(1,),
        start_index_map=(1,),
        operand_batching_dims=(0,),
        start_indices_batching_dims=(0,),
    )
    return lax.gather(
        row, classes[..., None], dimensions, (1, 1), mode=lax.GatherScatterMode.PROMISE_IN_BOUNDS
    )


def advance(a, b, total, coefficients_of, valid_rows):
    length, tiles = a.shape[1], a.shape[2]
    tile = (SUBLANES, LANES)
    lane = lax.broadcasted_iota(jnp.int32, tile, 1)
    block = lax.broadcasted_iota(jnp.int32, tile, 0)
    after_first, before_last = lane > 0, lane < LANES - 1
    zero = jnp.zeros(tile, jnp.float32)

    def doubled(above, middle, below):
        vertical = [above[h] + below[h] for h in range(tiles)]
        spread = [(corner_weight / edge_weight) * vertical[h] + middle[h] for h in range(tiles)]
        from_left = jnp.where(after_first, pltpu.roll(spread[tiles - 1], 1, 1), zero)
        from_right = jnp.where(before_last, pltpu.roll(spread[0], LANES - 1, 1), zero)
        result = []
        for h in range(tiles):
            left = spread[h - 1] if h else from_left
            right = spread[h + 1] if h + 1 < tiles else from_right
            result.append((left + right) + (vertical[h] - (middle[h] + middle[h])))
        return result

    def sweep(source, target, k, odd, first):
        def row_of(c, i):
            if i < 0:
                return [
                    jnp.where(block == 0, zero, pltpu.roll(source[c, length - 1, h], 1, 0))
                    for h in range(tiles)
                ]
            if i == length:
                return [
                    jnp.where(block == BLOCKS - 1, zero, pltpu.roll(source[c, 0, h], SUBLANES - 1, 0))
                    for h in range(tiles)
                ]
            return [source[c, i, h] for h in range(tiles)]

        coefficient_at = coefficients_of(k, odd)
        if first:
            start_at = coefficients_of(0, False)
        near = [(row_of(c, -1), row_of(c, 0)) for c in range(2)]
        for i in range(length):
            if valid_rows is not None:
                at = block * length + i
                inside = (at >= valid_rows[0]) & (at < valid_rows[1])
            values = []
            for c in range(2):
                above, middle = near[c]
                below = row_of(c, i + 1)
                near[c] = (middle, below)
                result = doubled(above, middle, below)
                for h in range(tiles):
                    value = 0.5 * result[h] if first else result[h] - (growth * growth) * target[c, i, h]
                    if valid_rows is not None:
                        value = jnp.where(inside, value, zero)
                    target[c, i, h] = value
                    result[h] = value
                values.append(result)
            for h in range(tiles):
                coefficient = coefficient_at(i, h)
                if first:
                    start = start_at(i, h)
                    sums = [start * source[c, i, h] for c in range(2)]
                else:
                    sums = [total[c, i, h] for c in range(2)]
                if odd:
                    total[0, i, h] = sums[0] - coefficient * values[1][h]
                    total[1, i, h] = sums[1] + coefficient * values[0][h]
                else:
                    total[0, i, h] = sums[0] + coefficient * values[0][h]
                    total[1, i, h] = sums[1] + coefficient * values[1][h]

    sweep(a, b, 1, True, True)

    def pair(n, carry):
        sweep(b, a, 2 * n, False, False)
        sweep(a, b, 2 * n + 1, True, False)
        return carry

    lax.fori_loop(1, TERMS // 2, pair, 0)


def looked_up(classes, table, turn, side):
    def coefficients_of(k, odd):
        row = table[turn, k]
        if odd:
            row = row * sign_of(side)
        return lambda i, h: pick(row, classes[i, h])

    return coefficients_of


def stored(ref):
    return lambda k, odd: lambda i, h: ref[k, i, h]


def coefficient_kernel(turn, blocks_ref, table_ref, out_ref):
    coefficients_of = looked_up(blocks_ref, table_ref, turn, lax.axis_index("lat"))
    for k in range(TERMS):
        coefficient_at = coefficients_of(k, k % 2 == 1)
        for i in range(out_ref.shape[1]):
            for h in range(out_ref.shape[2]):
                out_ref[k, i, h] = coefficient_at(i, h)


def picked(sources, indices, which):
    result = pick(sources[0], indices)
    for n in range(1, len(sources)):
        result = jnp.where(which == n, pick(sources[n], indices), result)
    return result


def interleaved(tiles_of, rows):
    tiles = len(tiles_of)
    lane = lax.broadcasted_iota(jnp.int32, (rows, LANES), 1)
    return [
        picked(tiles_of, (tiles * lane + j) % LANES, (tiles * lane + j) // LANES) for j in range(tiles)
    ]


def natural_order(tiles_of, rows):
    tiles = len(tiles_of)
    lane = lax.broadcasted_iota(jnp.int32, (rows, LANES), 1)
    return [
        picked(tiles_of, (LANES * t + lane) // tiles, (LANES * t + lane) % tiles) for t in range(tiles)
    ]


def sign_of(side):
    return jnp.where(side == 0, 1.0, -1.0).astype(jnp.float32)


def block_of(natural, c, i, h, length):
    return natural[h, pl.ds(PAD + c * BLOCKS * length + i, BLOCKS, stride=length), :]


def gather_blocks(natural, target):
    length = target.shape[1]
    for c in range(2):
        for i in range(length):
            for h in range(target.shape[2]):
                target[c, i, h] = block_of(natural, c, i, h, length)


PAD = 8


def windows(blocks, natural, own_ref, send_ref):
    side = lax.axis_index("lat")
    _, length, tiles, _, _ = blocks.shape
    rows = BLOCKS * length
    strip_rows = rows // 2
    for c in range(2):
        for i in range(length):
            for h in range(tiles):
                natural[h, pl.ds(PAD + c * rows + i, BLOCKS, stride=length), :] = blocks[c, i, h]
    for ref, strip in ((own_ref, side), (send_ref, 1 - side)):
        begin = strip * strip_rows - MARGIN
        for component in range(2):
            for r in range(0, strip_rows + 2 * MARGIN, SUBLANES):
                at = PAD + component * rows + begin + r
                found = [natural[h, pl.ds(at, SUBLANES), :] for h in range(tiles)]
                row = lax.broadcasted_iota(jnp.int32, (SUBLANES, LANES), 0) + (begin + r)
                inside = (row >= 0) & (row < rows)
                for h, part in enumerate(natural_order(found, SUBLANES)):
                    ref[component, h, r : r + SUBLANES, :] = jnp.where(inside, part, 0.0)


def window_kernel(blocks_ref, own_ref, send_ref, natural):
    windows(blocks_ref, natural, own_ref, send_ref)


def place(natural, source, component, rows, row):
    tiles = natural.shape[0]
    for r in range(0, source.shape[0], SUBLANES):
        parts = [source[r : r + SUBLANES, h * LANES : (h + 1) * LANES] for h in range(tiles)]
        at = pl.multiple_of(PAD + component * rows + row + r, 8)
        for h, part in enumerate(interleaved(parts, SUBLANES)):
            natural[h, pl.ds(at, SUBLANES), :] = part


def split_kernel(in_ref, class_ref, own_ref, send_ref, whole, whole_classes, sem):
    side = lax.axis_index("lat")
    fields = pltpu.make_async_copy(in_ref.at[0], whole, sem.at[0])
    cells = pltpu.make_async_copy(class_ref.at[0], whole_classes, sem.at[1])
    fields.start()
    cells.start()
    cells.wait()
    as_float = whole_classes[...].astype(jnp.float32)
    own_ref[2] = as_float
    send_ref[2] = as_float
    fields.wait()
    for component in range(2):
        own_ref[component] = whole[side * 2 + component]
        send_ref[component] = whole[(1 - side) * 2 + component]


def pack(strips, target):
    for component in range(2):
        for j in range(strips.shape[1] // SUBLANES):
            for h in range(target.shape[2]):
                at = (component, slice(j * SUBLANES, (j + 1) * SUBLANES), slice(h * LANES, (h + 1) * LANES))
                target[component, j, h] = strips[at]


def unpack(source, natural, component, rows, row, count):
    tiles = natural.shape[0]
    for j in range(count // SUBLANES):
        at = pl.multiple_of(PAD + component * rows + row + j * SUBLANES, 8)
        parts = [source[component, j, h] for h in range(tiles)]
        for h, part in enumerate(interleaved(parts, SUBLANES)):
            natural[h, pl.ds(at, SUBLANES), :] = part


def turn_of(turn, coefficients_of, a, b, enter_ref, strip, sem, hand_ref, cross_ref):
    side = lax.axis_index("lat")
    slab = lax.axis_index("depth")
    fetch = pltpu.make_async_copy(enter_ref.at[turn, pl.ds(2 * (1 - side), 2)], strip, sem)

    @pl.when(slab == 0)
    def _():
        fetch.start()

    advance(a, b, hand_ref, coefficients_of, None)

    @pl.when(slab == 0)
    def _():
        fetch.wait()
        pack(strip, cross_ref)

    @pl.when(slab > 0)
    def _():
        cross_ref[...] = hand_ref[...]


def first_kernel(own_ref, got_ref, table_ref, enter_ref, *rest):
    hand_ref, cross_ref, blocks_ref, a, b, natural, strip, sem = rest
    side = lax.axis_index("lat")
    strip_rows = own_ref.shape[1]
    rows = 2 * strip_rows
    length = a.shape[1]
    place(natural, own_ref[2], 0, rows, side * strip_rows)
    place(natural, got_ref[2], 0, rows, (1 - side) * strip_rows)
    for i in range(length):
        for h in range(a.shape[2]):
            blocks_ref[i, h] = block_of(natural, 0, i, h, length).astype(jnp.int32)
    for component in range(2):
        place(natural, own_ref[component], component, rows, side * strip_rows)
        place(natural, got_ref[component], component, rows, (1 - side) * strip_rows)
    gather_blocks(natural, a)
    turn_of(0, looked_up(blocks_ref, table_ref, 0, side), a, b, enter_ref, strip, sem.at[0], hand_ref, cross_ref)


def next_kernel(turn, plane, got_ref, crossed_ref, coefficient_ref, enter_ref, *rest):
    *outs, a, b, total, natural, strip, sem = rest
    side = lax.axis_index("lat")
    slab = lax.axis_index("depth")
    strip_rows = strip.shape[1]
    rows = 2 * strip_rows

    @pl.when(slab == 0)
    def _():
        fetch = pltpu.make_async_copy(enter_ref.at[turn - 1, pl.ds(2 * side, 2)], strip, sem.at[1])
        fetch.start()
        fetch.wait()
        for component in range(2):
            place(natural, strip[component], component, rows, side * strip_rows)
            unpack(crossed_ref, natural, component, rows, (1 - side) * strip_rows, strip_rows)
        gather_blocks(natural, a)

    @pl.when((slab > 0) & (slab % plane == 0))
    def _():
        a[...] = crossed_ref[...]

    @pl.when(slab % plane > 0)
    def _():
        a[...] = got_ref[...]

    if turn == TURNS - 1:
        advance(a, b, total, stored(coefficient_ref), None)
        windows(total, natural, *outs)
    else:
        turn_of(turn, stored(coefficient_ref), a, b, enter_ref, strip, sem.at[0], *outs)


def correlate(mine, got, strip_rows, images):
    sign = jnp.where(lax.axis_index("lat") == 0, 1, -1)
    tiles = mine[0].shape[1]
    for h in range(tiles):
        for o in range(OFFSETS):
            lag = sign * (o - MARGIN)
            total = None
            for ours, theirs in zip(mine, got):
                for component in range(2):
                    product = (
                        ours[component, h, pl.ds(MARGIN - lag, strip_rows), :]
                        * theirs[component, h, pl.ds(MARGIN + lag, strip_rows), :]
                    )
                    total = product if total is None else total + product
            images(o, h, total)


def early_kernel(*refs):
    *pairs, out_ref = refs

    def images(o, h, total):
        out_ref[o, h] = total

    correlate(pairs[0::2], pairs[1::2], out_ref.shape[2], images)


def image_kernel(early_ref, mine_ref, got_ref, images_out, wave_out, images_ref, wave_ref, sem):
    side = lax.axis_index("lat")
    strip_rows = wave_ref.shape[1]
    tiles = mine_ref.shape[1]
    rows = slice(MARGIN, MARGIN + strip_rows)
    for j, (ref, which) in enumerate(((mine_ref, side), (got_ref, 1 - side))):
        for component in range(2):
            for h in range(tiles):
                wave_ref[2 * which + component, :, h * LANES : (h + 1) * LANES] = ref[component, h, rows, :]
    copies = [pltpu.make_async_copy(wave_ref, wave_out.at[0], sem.at[0])]
    copies[0].start()
    done = []

    def images(o, h, total):
        images_ref[h, o] = early_ref[o, h] + total
        done.append(o)
        if len(done) % OFFSETS == 0:
            copy = pltpu.make_async_copy(
                images_ref.at[h], images_out.at[0, :, :, pl.ds(h * LANES, LANES)], sem.at[1 + h]
            )
            copy.start()
            copies.append(copy)

    correlate([mine_ref], [got_ref], strip_rows, images)
    for copy in copies:
        copy.wait()


def field_scratch(length, tiles):
    return [pltpu.VMEM((2, length, tiles, BLOCKS, LANES), jnp.float32)] * 2


def coefficients(freq_phase, class_slowness):
    (table,) = call(
        table_kernel,
        [f32(TURNS, TERMS, SUBLANES, LANES)],
        [HBM, HBM],
        [
            pltpu.VMEM((SUBLANES, LANES), jnp.float32),
            pltpu.SMEM(freq_phase.shape, jnp.float32),
            pltpu.VMEM((1, class_slowness.shape[0]), jnp.float32),
            pltpu.SemaphoreType.DMA((2,)),
        ],
        in_hbm(freq_phase, class_slowness.reshape(1, -1)),
    )
    return table


def paired(in_flight, entering, classes, freq_phase, class_slowness):
    depth = lax.axis_size("depth")
    _, _, strip_rows, width = in_flight.shape
    tiles = width // LANES
    length = 2 * strip_rows // BLOCKS
    swap = [(0, 1), (1, 0)]
    plane = PLANE if depth % PLANE == 0 else depth
    ring = [(i, i - i % plane + (i + 1) % plane) for i in range(depth)]
    across = {}
    for first in range(plane, depth, plane):
        across[first - 1], across[first] = first, first - 1
    cross = [
        (2 * d + c, 2 * across[d] + c if d in across else 2 * d + 1 - c)
        for d in range(depth)
        for c in range(2)
    ]
    blocks = f32(2, length, tiles, BLOCKS, LANES)
    window = f32(2, tiles, strip_rows + 2 * MARGIN, LANES)
    natural = pltpu.VMEM((tiles, 2 * BLOCKS * length + 2 * PAD, LANES), jnp.float32)
    scratch = field_scratch(length, tiles) + [
        natural,
        pltpu.VMEM((2, strip_rows, width), jnp.float32),
        pltpu.SemaphoreType.DMA((2,)),
    ]
    strips = f32(3, strip_rows, width)
    flops = 20 * TERMS * 4 * strip_rows * width

    own, send = call(
        split_kernel,
        [strips, strips],
        [HBM, HBM],
        [
            pltpu.VMEM((4, strip_rows, width), jnp.float32),
            pltpu.VMEM((strip_rows, width), jnp.int32),
            pltpu.SemaphoreType.DMA((2,)),
        ],
        in_hbm(in_flight, classes),
    )
    got = lax.ppermute(send, "lat", swap)
    freq_phase, _ = lax.optimization_barrier((freq_phase, own))
    table = coefficients(freq_phase, class_slowness)
    hand, over, cells = call(
        first_kernel,
        [blocks, blocks, jax.ShapeDtypeStruct(blocks.shape[1:], jnp.int32)],
        [VMEM, VMEM, VMEM, HBM],
        scratch,
        (own, got, table, entering),
        flops,
    )
    pairs = []
    for turn in range(1, TURNS):
        handed = lax.ppermute(hand, "depth", ring)
        crossed = lax.ppermute(over, ("depth", "lat"), cross)
        mine, send = call(window_kernel, [window, window], [VMEM], [natural], (hand,))
        pairs += [mine, lax.ppermute(send, "lat", swap)]
        last = turn == TURNS - 1
        (coefficient,) = call(
            functools.partial(coefficient_kernel, turn),
            [f32(TERMS, *blocks.shape[1:])],
            [VMEM] * 2,
            [],
            (cells, table),
        )
        hand, over = call(
            functools.partial(next_kernel, turn, plane),
            [window, window] if last else [blocks, blocks],
            [VMEM, VMEM, VMEM, HBM],
            scratch[:2] + [scratch[0]] + scratch[2:],
            (handed, crossed, coefficient, entering),
            flops,
        )
    mine, send = hand, over
    got = lax.ppermute(send, "lat", swap)
    (early,) = call(
        early_kernel,
        [f32(OFFSETS, tiles, strip_rows, LANES)],
        [VMEM] * len(pairs),
        [],
        pairs,
    )
    return tuple(
        call(
            image_kernel,
            [f32(1, OFFSETS, strip_rows, width), f32(1, 4, strip_rows, width)],
            [VMEM] * 3,
            [
                pltpu.VMEM((tiles, OFFSETS, strip_rows, LANES), jnp.float32),
                pltpu.VMEM((4, strip_rows, width), jnp.float32),
                pltpu.SemaphoreType.DMA((1 + tiles,)),
            ],
            (early, mine, got),
            out_specs=[HBM] * 2,
        )
    )


def inside_kernel(turn, limits_ref, field_ref, blocks_ref, table_ref, out_ref, a, b):
    a[...] = field_ref[...]
    side = lax.axis_index("lat") % 2
    valid = (limits_ref[0], limits_ref[1])
    advance(a, b, out_ref, looked_up(blocks_ref, table_ref, turn, side), valid)


def grouped(in_flight, entering, classes, freq_phase, class_slowness):
    depth, strips = lax.axis_size("depth"), lax.axis_size("lat")
    strip = lax.axis_index("lat")
    side, group = strip % 2, strip // 2
    _, _, strip_rows, width = in_flight.shape
    tiles = width // LANES
    core = 2 * strip_rows
    halo = TERMS - 1 + MARGIN
    while (core + 2 * halo) % BLOCKS:
        halo += 1
    rows = core + 2 * halo
    length = rows // BLOCKS
    swap = [(i, i ^ 1) for i in range(strips)]
    shift = [(i, i + 1) for i in range(depth - 1)]
    blocks = f32(2, length, tiles, BLOCKS, LANES)

    def both_strips(mine, sent):
        got = lax.ppermute(sent, "lat", swap)
        return jnp.where(
            side == 0, jnp.concatenate([mine, got], 1), jnp.concatenate([got, mine], 1)
        )

    def own_components(fields):
        return both_strips(
            lax.dynamic_slice_in_dim(fields, 2 * side, 2, 0),
            lax.dynamic_slice_in_dim(fields, 2 * (1 - side), 2, 0),
        )

    def with_halo(cells):
        above = lax.ppermute(cells[:, core - halo :], "lat", [(i, i + 2) for i in range(strips - 2)])
        below = lax.ppermute(cells[:, :halo], "lat", [(i + 2, i) for i in range(strips - 2)])
        return jnp.concatenate([above, cells, below], 1)

    def to_blocks(cells):
        split = cells.reshape(-1, BLOCKS, length, LANES, tiles)
        return split.transpose(0, 2, 4, 1, 3)

    def to_rows(cells):
        return cells.transpose(0, 3, 1, 4, 2).reshape(2, rows, width)

    def window(cells, which):
        begin = halo - MARGIN + which * strip_rows
        return lax.dynamic_slice_in_dim(cells, begin, strip_rows + 2 * MARGIN, 1)

    cells = to_blocks(with_halo(both_strips(classes, classes)))[0]
    table = coefficients(freq_phase, class_slowness)
    before = group * core - halo
    limits = jnp.stack([jnp.maximum(-before, 0), jnp.minimum(strips * strip_rows - before, rows)])
    field = own_components(in_flight[0])
    images = jnp.zeros((OFFSETS, strip_rows, width), jnp.float32)
    for turn in range(TURNS):
        (advanced,) = call(
            functools.partial(inside_kernel, turn),
            [blocks],
            [SMEM, VMEM, VMEM, VMEM],
            field_scratch(length, tiles),
            (limits.astype(jnp.int32), to_blocks(with_halo(field)), cells, table),
        )
        advanced = to_rows(advanced)
        mine = window(advanced, side)
        got = lax.ppermute(window(advanced, 1 - side), "lat", swap)
        source, receiver = jnp.where(side == 0, mine, got), jnp.where(side == 0, got, mine)
        products = []
        for o in range(OFFSETS):
            lag = o - MARGIN
            first = source[:, MARGIN - lag : MARGIN - lag + strip_rows]
            second = receiver[:, MARGIN + lag : MARGIN + lag + strip_rows]
            products.append(first[0] * second[0] + first[1] * second[1])
        images = images + jnp.stack(products)
        if turn + 1 < TURNS:
            handed = lax.ppermute(advanced[:, halo : halo + core], "depth", shift)
            entered = own_components(entering[turn])
            field = jnp.where(lax.axis_index("depth") == 0, entered, handed)
    own = slice(MARGIN, MARGIN + strip_rows)
    return images[None], jnp.concatenate([source[:, own], receiver[:, own]], 0)[None]


def solution(mesh):
    in_specs = (
        P("depth", None, "lat", None),
        P(None, None, "lat", None),
        P("depth", "lat", None),
        P(),
        P(),
    )
    out_specs = (P("depth", None, "lat", None), P("depth", None, "lat", None))
    local = paired if mesh.shape["lat"] == 2 else grouped
    return jax.shard_map(local, mesh=mesh, in_specs=in_specs, out_specs=out_specs, check_vma=False)
```

```python
import functools

import jax
import jax.numpy as jnp
from jax import lax
from jax.experimental import pallas as pl
from jax.experimental.pallas import tpu as pltpu
from jax.sharding import PartitionSpec as P

TERMS = 16
OFFSETS = 8
TURNS = 3
LANES = 128
SUBLANES = 8
PLANE = 4
BLOCKS = 8
MARGIN = OFFSETS // 2
VMEM_BYTES = 4 << 20

hale_weight = 0.0255
edge_weight = 0.25 - 0.5 * hale_weight
corner_weight = 0.125 + 0.25 * hale_weight
growth = 1.0 / (2.0 * edge_weight)
miller_start = 32

VMEM = pl.BlockSpec(memory_space=pltpu.VMEM)
SMEM = pl.BlockSpec(memory_space=pltpu.SMEM)
HBM = pl.BlockSpec(memory_space=pltpu.HBM)
ANY = pl.BlockSpec(memory_space=pl.ANY)


def call(kernel, outs, in_specs, scratch, args, flops=0, out_specs=None):
    moved = 4 * sum(int(a.size) for a in (*args, *outs))
    return pl.pallas_call(
        kernel,
        out_shape=outs,
        in_specs=in_specs,
        out_specs=out_specs or [VMEM] * len(outs),
        scratch_shapes=scratch,
        compiler_params=pltpu.CompilerParams(vmem_limit_bytes=VMEM_BYTES),
        cost_estimate=pl.CostEstimate(flops=flops, bytes_accessed=moved, transcendentals=0),
    )(*args)


def in_hbm(*arrays):
    return tuple(pltpu.with_memory_space_constraint(x, pltpu.HBM) for x in arrays)


def f32(*shape):
    return jax.ShapeDtypeStruct(shape, jnp.float32)


def table_kernel(phase_hbm, slow_hbm, out_ref, z_ref, phase_ref, slow_ref, sem):
    copies = [
        pltpu.make_async_copy(phase_hbm, phase_ref, sem.at[0]),
        pltpu.make_async_copy(slow_hbm, slow_ref, sem.at[1]),
    ]
    for copy in copies:
        copy.start()
    for copy in copies:
        copy.wait()
    first = lax.axis_size("depth") - 1 - lax.axis_index("depth")
    classes = slow_ref.shape[1]
    z_ref[...] = jnp.full(z_ref.shape, 6.0, jnp.float32)
    for turn in range(TURNS):
        z_ref[turn : turn + 1, 0:classes] = slow_ref[...] * phase_ref[first + turn]
    phases = z_ref[...]
    values = [None] * (miller_start + 1)
    upper = jnp.zeros_like(phases)
    current = jnp.ones_like(phases)
    values[miller_start] = current
    inverse = 1.0 / phases
    for k in range(miller_start, 0, -1):
        lower = (2.0 * k * inverse) * current - upper
        values[k - 1] = lower
        upper, current = current, lower
    evens = values[2]
    for k in range(4, miller_start + 1, 2):
        evens = evens + values[k]
    scale = 1.0 / (values[0] + 2.0 * evens)
    for k in range(TERMS):
        factor = (1.0 if k == 0 else 2.0) * (1.0 if k % 4 < 2 else -1.0) * growth**-k
        ratio = values[k] * scale * factor
        for turn in range(TURNS):
            out_ref[turn, k] = jnp.broadcast_to(ratio[turn : turn + 1, :], (SUBLANES, LANES))


def pick(row, classes):
    dimensions = lax.GatherDimensionNumbers(
        offset_dims=(),
        collapsed_slice_dims=(1,),
        start_index_map=(1,),
        operand_batching_dims=(0,),
        start_indices_batching_dims=(0,),
    )
    return lax.gather(
        row, classes[..., None], dimensions, (1, 1), mode=lax.GatherScatterMode.PROMISE_IN_BOUNDS
    )


def advance(a, b, total, coefficients_of, valid_rows):
    length, tiles = a.shape[1], a.shape[2]
    tile = (SUBLANES, LANES)
    lane = lax.broadcasted_iota(jnp.int32, tile, 1)
    block = lax.broadcasted_iota(jnp.int32, tile, 0)
    after_first, before_last = lane > 0, lane < LANES - 1
    zero = jnp.zeros(tile, jnp.float32)

    def doubled(above, middle, below):
        vertical = [above[h] + below[h] for h in range(tiles)]
        spread = [(corner_weight / edge_weight) * vertical[h] + middle[h] for h in range(tiles)]
        from_left = jnp.where(after_first, pltpu.roll(spread[tiles - 1], 1, 1), zero)
        from_right = jnp.where(before_last, pltpu.roll(spread[0], LANES - 1, 1), zero)
        result = []
        for h in range(tiles):
            left = spread[h - 1] if h else from_left
            right = spread[h + 1] if h + 1 < tiles else from_right
            result.append((left + right) + (vertical[h] - (middle[h] + middle[h])))
        return result

    def sweep(source, target, k, odd, first):
        def row_of(c, i):
            if i < 0:
                return [
                    jnp.where(block == 0, zero, pltpu.roll(source[c, length - 1, h], 1, 0))
                    for h in range(tiles)
                ]
            if i == length:
                return [
                    jnp.where(block == BLOCKS - 1, zero, pltpu.roll(source[c, 0, h], SUBLANES - 1, 0))
                    for h in range(tiles)
                ]
            return [source[c, i, h] for h in range(tiles)]

        coefficient_at = coefficients_of(k, odd)
        if first:
            start_at = coefficients_of(0, False)
        near = [(row_of(c, -1), row_of(c, 0)) for c in range(2)]
        for i in range(length):
            if valid_rows is not None:
                at = block * length + i
                inside = (at >= valid_rows[0]) & (at < valid_rows[1])
            values = []
            for c in range(2):
                above, middle = near[c]
                below = row_of(c, i + 1)
                near[c] = (middle, below)
                result = doubled(above, middle, below)
                for h in range(tiles):
                    value = 0.5 * result[h] if first else result[h] - (growth * growth) * target[c, i, h]
                    if valid_rows is not None:
                        value = jnp.where(inside, value, zero)
                    target[c, i, h] = value
                    result[h] = value
                values.append(result)
            for h in range(tiles):
                coefficient = coefficient_at(i, h)
                if first:
                    start = start_at(i, h)
                    sums = [start * source[c, i, h] for c in range(2)]
                else:
                    sums = [total[c, i, h] for c in range(2)]
                if odd:
                    total[0, i, h] = sums[0] - coefficient * values[1][h]
                    total[1, i, h] = sums[1] + coefficient * values[0][h]
                else:
                    total[0, i, h] = sums[0] + coefficient * values[0][h]
                    total[1, i, h] = sums[1] + coefficient * values[1][h]

    sweep(a, b, 1, True, True)

    def pair(n, carry):
        sweep(b, a, 2 * n, False, False)
        sweep(a, b, 2 * n + 1, True, False)
        return carry

    lax.fori_loop(1, TERMS // 2, pair, 0)


def looked_up(classes, table, turn, side):
    def coefficients_of(k, odd):
        row = table[turn, k]
        if odd:
            row = row * sign_of(side)
        return lambda i, h: pick(row, classes[i, h])

    return coefficients_of


def stored(ref):
    return lambda k, odd: lambda i, h: ref[k, i, h]


def coefficient_kernel(turn, blocks_ref, table_ref, out_ref):
    coefficients_of = looked_up(blocks_ref, table_ref, turn, lax.axis_index("lat"))
    for k in range(TERMS):
        coefficient_at = coefficients_of(k, k % 2 == 1)
        for i in range(out_ref.shape[1]):
            for h in range(out_ref.shape[2]):
                out_ref[k, i, h] = coefficient_at(i, h)


def picked(sources, indices, which):
    result = pick(sources[0], indices)
    for n in range(1, len(sources)):
        result = jnp.where(which == n, pick(sources[n], indices), result)
    return result


def interleaved(tiles_of, rows):
    tiles = len(tiles_of)
    lane = lax.broadcasted_iota(jnp.int32, (rows, LANES), 1)
    return [
        picked(tiles_of, (tiles * lane + j) % LANES, (tiles * lane + j) // LANES) for j in range(tiles)
    ]


def natural_order(tiles_of, rows):
    tiles = len(tiles_of)
    lane = lax.broadcasted_iota(jnp.int32, (rows, LANES), 1)
    return [
        picked(tiles_of, (LANES * t + lane) // tiles, (LANES * t + lane) % tiles) for t in range(tiles)
    ]


def sign_of(side):
    return jnp.where(side == 0, 1.0, -1.0).astype(jnp.float32)


def block_of(natural, c, i, h, length):
    return natural[h, pl.ds(PAD + c * BLOCKS * length + i, BLOCKS, stride=length), :]


def gather_blocks(natural, target):
    length = target.shape[1]
    for c in range(2):
        for i in range(length):
            for h in range(target.shape[2]):
                target[c, i, h] = block_of(natural, c, i, h, length)


PAD = 8


def windows(blocks, natural, own_ref, send_ref):
    side = lax.axis_index("lat")
    _, length, tiles, _, _ = blocks.shape
    rows = BLOCKS * length
    strip_rows = rows // 2
    for c in range(2):
        for i in range(length):
            for h in range(tiles):
                natural[h, pl.ds(PAD + c * rows + i, BLOCKS, stride=length), :] = blocks[c, i, h]
    for ref, strip in ((own_ref, side), (send_ref, 1 - side)):
        begin = strip * strip_rows - MARGIN
        for component in range(2):
            for r in range(0, strip_rows + 2 * MARGIN, SUBLANES):
                at = PAD + component * rows + begin + r
                found = [natural[h, pl.ds(at, SUBLANES), :] for h in range(tiles)]
                row = lax.broadcasted_iota(jnp.int32, (SUBLANES, LANES), 0) + (begin + r)
                inside = (row >= 0) & (row < rows)
                for h, part in enumerate(natural_order(found, SUBLANES)):
                    ref[component, h, r : r + SUBLANES, :] = jnp.where(inside, part, 0.0)


def window_kernel(blocks_ref, *rest):
    *before, own_ref, send_ref, natural = rest
    for ref in before:
        send_ref[: ref.shape[0]] = ref[...]
    windows(blocks_ref, natural, own_ref, send_ref.at[send_ref.shape[0] - 1])


def place(natural, source, component, rows, row):
    tiles = natural.shape[0]
    for r in range(0, source.shape[0], SUBLANES):
        parts = [source[r : r + SUBLANES, h * LANES : (h + 1) * LANES] for h in range(tiles)]
        at = pl.multiple_of(PAD + component * rows + row + r, 8)
        for h, part in enumerate(interleaved(parts, SUBLANES)):
            natural[h, pl.ds(at, SUBLANES), :] = part


def split_kernel(in_ref, class_ref, own_ref, send_ref, whole_classes, sem):
    side = lax.axis_index("lat")
    cells = pltpu.make_async_copy(class_ref.at[0], whole_classes, sem.at[0])
    cells.start()
    copies = [
        pltpu.make_async_copy(in_ref.at[0, pl.ds(2 * which, 2)], ref.at[pl.ds(0, 2)], sem.at[j])
        for j, (ref, which) in enumerate(((send_ref, 1 - side), (own_ref, side)), 1)
    ]
    for copy in copies:
        copy.start()
    cells.wait()
    as_float = whole_classes[...].astype(jnp.float32)
    own_ref[2] = as_float
    send_ref[2] = as_float
    for copy in copies:
        copy.wait()


def pack(fields, first, target):
    count = fields.shape[2] // SUBLANES
    for turn in range(TURNS - 1):
        for component in range(2):
            for j in range(count):
                for h in range(target.shape[2]):
                    rows, at = slice(j * SUBLANES, (j + 1) * SUBLANES), slice(h * LANES, (h + 1) * LANES)
                    target[component, turn * count + j, h] = fields[turn, first + component, rows, at]


def unpack(source, turn, natural, component, rows, row):
    tiles = natural.shape[0]
    count = source.shape[1] // (TURNS - 1)
    for j in range(count):
        at = pl.multiple_of(PAD + component * rows + row + j * SUBLANES, 8)
        parts = [source[component, turn * count + j, h] for h in range(tiles)]
        for h, part in enumerate(interleaved(parts, SUBLANES)):
            natural[h, pl.ds(at, SUBLANES), :] = part


def weave_kernel(strips_ref, out_ref):
    tiles = out_ref.shape[1]
    for n in range(strips_ref.shape[0]):
        for r in range(0, strips_ref.shape[1], SUBLANES):
            parts = [
                strips_ref[n, r : r + SUBLANES, h * LANES : (h + 1) * LANES] for h in range(tiles)
            ]
            for h, part in enumerate(interleaved(parts, SUBLANES)):
                out_ref[n, h, r : r + SUBLANES, :] = part


def lay(natural, woven, component, rows, row):
    tiles, count = woven.shape[:2]
    for h in range(tiles):
        at = pl.multiple_of(PAD + component * rows + row, 8)
        natural[h, pl.ds(at, count), :] = woven[h]


def first_kernel(own_ref, got_ref, table_ref, enter_ref, *rest):
    hand_ref, cross_ref, blocks_ref, a, b, natural = rest
    side = lax.axis_index("lat")
    strip_rows = got_ref.shape[1]
    rows = 2 * strip_rows
    length = a.shape[1]
    lay(natural, own_ref[2], 0, rows, side * strip_rows)
    place(natural, got_ref[2], 0, rows, (1 - side) * strip_rows)
    for i in range(length):
        for h in range(a.shape[2]):
            blocks_ref[i, h] = block_of(natural, 0, i, h, length).astype(jnp.int32)
    for component in range(2):
        lay(natural, own_ref[component], component, rows, side * strip_rows)
        place(natural, got_ref[component], component, rows, (1 - side) * strip_rows)
    gather_blocks(natural, a)
    advance(a, b, hand_ref, looked_up(blocks_ref, table_ref, 0, side), None)
    top = lax.axis_index("depth") == 0

    @pl.when(top)
    def _():
        pack(enter_ref, 2 * (1 - side), cross_ref)

    @pl.when(jnp.logical_not(top))
    def _():
        cross_ref[...] = hand_ref[...]


def next_kernel(turn, plane, got_ref, crossed_ref, entered_ref, coefficient_ref, enter_ref, *rest):
    *outs, a, b, total, natural = rest
    side = lax.axis_index("lat")
    slab = lax.axis_index("depth")
    strip_rows = enter_ref.shape[2]
    rows = 2 * strip_rows

    @pl.when(slab == 0)
    def _():
        for component in range(2):
            place(natural, enter_ref[turn - 1, 2 * side + component], component, rows, side * strip_rows)
            unpack(entered_ref, turn - 1, natural, component, rows, (1 - side) * strip_rows)
        gather_blocks(natural, a)

    @pl.when((slab > 0) & (slab % plane == 0))
    def _():
        a[...] = crossed_ref[...]

    @pl.when(slab % plane > 0)
    def _():
        a[...] = got_ref[...]

    if turn == TURNS - 1:
        advance(a, b, total, stored(coefficient_ref), None)
        windows(total, natural, *outs)
    else:
        advance(a, b, outs[0], stored(coefficient_ref), None)


def correlate(mine, got, strip_rows, images):
    sign = jnp.where(lax.axis_index("lat") == 0, 1, -1)
    tiles = mine[0].shape[1]
    for h in range(tiles):
        for o in range(OFFSETS):
            lag = sign * (o - MARGIN)
            total = None
            for ours, theirs in zip(mine, got):
                for component in range(2):
                    product = (
                        ours[component, h, pl.ds(MARGIN - lag, strip_rows), :]
                        * theirs[component, h, pl.ds(MARGIN + lag, strip_rows), :]
                    )
                    total = product if total is None else total + product
            images(o, h, total)


def early_kernel(*refs):
    *ours, theirs, out_ref = refs

    def images(o, h, total):
        out_ref[o, h] = total

    correlate(ours, [theirs.at[t] for t in range(len(ours))], out_ref.shape[2], images)


def image_kernel(early_ref, mine_ref, got_ref, images_out, wave_out, images_ref, wave_ref, sem):
    side = lax.axis_index("lat")
    strip_rows = wave_ref.shape[1]
    tiles = mine_ref.shape[1]
    rows = slice(MARGIN, MARGIN + strip_rows)
    for ref, which in ((mine_ref, side), (got_ref, 1 - side)):
        for component in range(2):
            for h in range(tiles):
                wave_ref[2 * which + component, :, h * LANES : (h + 1) * LANES] = ref[component, h, rows, :]
    copies = [pltpu.make_async_copy(wave_ref, wave_out.at[0], sem.at[0])]
    copies[0].start()
    done = []

    def images(o, h, total):
        images_ref[h, o] = early_ref[o, h] + total
        done.append(o)
        if len(done) % OFFSETS == 0:
            copy = pltpu.make_async_copy(
                images_ref.at[h], images_out.at[0, :, :, pl.ds(h * LANES, LANES)], sem.at[1 + h]
            )
            copy.start()
            copies.append(copy)

    correlate([mine_ref], [got_ref], strip_rows, images)
    for copy in copies:
        copy.wait()


def field_scratch(length, tiles):
    return [pltpu.VMEM((2, length, tiles, BLOCKS, LANES), jnp.float32)] * 2


def coefficients(freq_phase, class_slowness):
    (table,) = call(
        table_kernel,
        [f32(TURNS, TERMS, SUBLANES, LANES)],
        [HBM, HBM],
        [
            pltpu.VMEM((SUBLANES, LANES), jnp.float32),
            pltpu.SMEM(freq_phase.shape, jnp.float32),
            pltpu.VMEM((1, class_slowness.shape[0]), jnp.float32),
            pltpu.SemaphoreType.DMA((2,)),
        ],
        in_hbm(freq_phase, class_slowness.reshape(1, -1)),
    )
    return table


def paired(in_flight, entering, classes, freq_phase, class_slowness):
    depth = lax.axis_size("depth")
    _, _, strip_rows, width = in_flight.shape
    tiles = width // LANES
    length = 2 * strip_rows // BLOCKS
    swap = [(0, 1), (1, 0)]
    plane = PLANE if depth % PLANE == 0 else depth
    ring = [(i, i - i % plane + (i + 1) % plane) for i in range(depth)]
    across, spare = {}, []
    for first in range(plane, depth, plane):
        across[first - 1], across[first], across[first + 2] = first, first + 2, first - 1
        spare.append(first + 1)

    def crossing(pairs):
        ways = dict(across)
        if across:
            for one, other in (*pairs, *zip(spare[0::2], spare[1::2])):
                ways[one], ways[other] = other, one
        return [(2 * d + c, 2 * ways[d] + c if d in ways else 2 * d + 1 - c) for d in range(depth) for c in range(2)]

    cross = {1: crossing([(1, 2)]), 2: crossing([(0, 1)])}
    blocks = f32(2, length, tiles, BLOCKS, LANES)
    window = f32(2, tiles, strip_rows + 2 * MARGIN, LANES)
    natural = pltpu.VMEM((tiles, 2 * BLOCKS * length + 2 * PAD, LANES), jnp.float32)
    scratch = field_scratch(length, tiles) + [natural]
    strips = f32(3, strip_rows, width)
    flops = 20 * TERMS * 4 * strip_rows * width

    own, send = call(
        split_kernel,
        [strips, strips],
        [HBM, HBM],
        [pltpu.VMEM((strip_rows, width), jnp.int32), pltpu.SemaphoreType.DMA((3,))],
        in_hbm(in_flight, classes),
    )
    got = lax.ppermute(send, "lat", swap)
    freq_phase, _ = lax.optimization_barrier((freq_phase, own))
    (own,) = call(weave_kernel, [f32(3, tiles, strip_rows, LANES)], [VMEM], [], (own,))
    table = coefficients(freq_phase, class_slowness)
    hand, over, cells = call(
        first_kernel,
        [blocks, blocks, jax.ShapeDtypeStruct(blocks.shape[1:], jnp.int32)],
        [VMEM, VMEM, VMEM, VMEM],
        scratch,
        (own, got, table, entering),
        flops,
    )
    mines, sent, coefficient = [], (), {}
    for turn in range(1, TURNS):
        handed = lax.ppermute(hand, "depth", ring)
        crossed = lax.ppermute(over, ("depth", "lat"), cross[min(turn, 2)])
        if turn == 1:
            entered = crossed
        mine, send = call(
            window_kernel,
            [window, f32(turn, *window.shape)],
            [VMEM] * (1 + len(sent)),
            [natural],
            (hand, *sent),
        )
        mines.append(mine)
        if turn == 1:
            for later in range(1, TURNS):
                (coefficient[later],) = call(
                    functools.partial(coefficient_kernel, later),
                    [f32(TERMS, *blocks.shape[1:])],
                    [VMEM] * 2,
                    [],
                    (cells, table),
                )
            coefficient[1], send, *others = lax.optimization_barrier(
                (coefficient[1], send, *(coefficient[later] for later in range(2, TURNS)))
            )
            coefficient.update(zip(range(2, TURNS), others))
        sent = (send,)
        last = turn == TURNS - 1
        outs = call(
            functools.partial(next_kernel, turn, plane),
            [window, window] if last else [blocks],
            [VMEM] * 5,
            scratch[:2] + [scratch[0]] + scratch[2:],
            (handed, crossed, entered, coefficient[turn], entering),
            flops,
        )
        hand = over = outs[0]
    earlier = lax.ppermute(send, "lat", swap)
    mine, send = outs
    got = lax.ppermute(send, "lat", swap)
    (early,) = call(
        early_kernel,
        [f32(OFFSETS, tiles, strip_rows, LANES)],
        [VMEM] * TURNS,
        [],
        (*mines, earlier),
    )
    return tuple(
        call(
            image_kernel,
            [f32(1, OFFSETS, strip_rows, width), f32(1, 4, strip_rows, width)],
            [VMEM] * 3,
            [
                pltpu.VMEM((tiles, OFFSETS, strip_rows, LANES), jnp.float32),
                pltpu.VMEM((4, strip_rows, width), jnp.float32),
                pltpu.SemaphoreType.DMA((1 + tiles,)),
            ],
            (early, mine, got),
            out_specs=[HBM] * 2,
        )
    )


def inside_kernel(turn, limits_ref, field_ref, blocks_ref, table_ref, out_ref, a, b):
    a[...] = field_ref[...]
    side = lax.axis_index("lat") % 2
    valid = (limits_ref[0], limits_ref[1])
    advance(a, b, out_ref, looked_up(blocks_ref, table_ref, turn, side), valid)


def grouped(in_flight, entering, classes, freq_phase, class_slowness):
    depth, strips = lax.axis_size("depth"), lax.axis_size("lat")
    strip = lax.axis_index("lat")
    side, group = strip % 2, strip // 2
    _, _, strip_rows, width = in_flight.shape
    tiles = width // LANES
    core = 2 * strip_rows
    halo = TERMS - 1 + MARGIN
    while (core + 2 * halo) % BLOCKS:
        halo += 1
    rows = core + 2 * halo
    length = rows // BLOCKS
    swap = [(i, i ^ 1) for i in range(strips)]
    shift = [(i, i + 1) for i in range(depth - 1)]
    blocks = f32(2, length, tiles, BLOCKS, LANES)

    def both_strips(mine, sent):
        got = lax.ppermute(sent, "lat", swap)
        return jnp.where(
            side == 0, jnp.concatenate([mine, got], 1), jnp.concatenate([got, mine], 1)
        )

    def own_components(fields):
        return both_strips(
            lax.dynamic_slice_in_dim(fields, 2 * side, 2, 0),
            lax.dynamic_slice_in_dim(fields, 2 * (1 - side), 2, 0),
        )

    def with_halo(cells):
        above = lax.ppermute(cells[:, core - halo :], "lat", [(i, i + 2) for i in range(strips - 2)])
        below = lax.ppermute(cells[:, :halo], "lat", [(i + 2, i) for i in range(strips - 2)])
        return jnp.concatenate([above, cells, below], 1)

    def to_blocks(cells):
        split = cells.reshape(-1, BLOCKS, length, LANES, tiles)
        return split.transpose(0, 2, 4, 1, 3)

    def to_rows(cells):
        return cells.transpose(0, 3, 1, 4, 2).reshape(2, rows, width)

    def window(cells, which):
        begin = halo - MARGIN + which * strip_rows
        return lax.dynamic_slice_in_dim(cells, begin, strip_rows + 2 * MARGIN, 1)

    cells = to_blocks(with_halo(both_strips(classes, classes)))[0]
    table = coefficients(freq_phase, class_slowness)
    before = group * core - halo
    limits = jnp.stack([jnp.maximum(-before, 0), jnp.minimum(strips * strip_rows - before, rows)])
    field = own_components(in_flight[0])
    images = jnp.zeros((OFFSETS, strip_rows, width), jnp.float32)
    for turn in range(TURNS):
        (advanced,) = call(
            functools.partial(inside_kernel, turn),
            [blocks],
            [SMEM, VMEM, VMEM, VMEM],
            field_scratch(length, tiles),
            (limits.astype(jnp.int32), to_blocks(with_halo(field)), cells, table),
        )
        advanced = to_rows(advanced)
        mine = window(advanced, side)
        got = lax.ppermute(window(advanced, 1 - side), "lat", swap)
        source, receiver = jnp.where(side == 0, mine, got), jnp.where(side == 0, got, mine)
        products = []
        for o in range(OFFSETS):
            lag = o - MARGIN
            first = source[:, MARGIN - lag : MARGIN - lag + strip_rows]
            second = receiver[:, MARGIN + lag : MARGIN + lag + strip_rows]
            products.append(first[0] * second[0] + first[1] * second[1])
        images = images + jnp.stack(products)
        if turn + 1 < TURNS:
            handed = lax.ppermute(advanced[:, halo : halo + core], "depth", shift)
            entered = own_components(entering[turn])
            field = jnp.where(lax.axis_index("depth") == 0, entered, handed)
    own = slice(MARGIN, MARGIN + strip_rows)
    return images[None], jnp.concatenate([source[:, own], receiver[:, own]], 0)[None]


def solution(mesh):
    in_specs = (
        P("depth", None, "lat", None),
        P(None, None, "lat", None),
        P("depth", "lat", None),
        P(),
        P(),
    )
    out_specs = (P("depth", None, "lat", None), P("depth", None, "lat", None))
    pair = mesh.shape["lat"] == 2
    local = paired if pair else grouped
    return jax.shard_map(local, mesh=mesh, in_specs=in_specs, out_specs=out_specs, check_vma=False)
```

```python
import functools

import jax
import jax.numpy as jnp
from jax import lax
from jax.experimental import pallas as pl
from jax.experimental.pallas import tpu as pltpu
from jax.sharding import PartitionSpec as P

TERMS = 16
OFFSETS = 8
TURNS = 3
LANES = 128
SUBLANES = 8
PLANE = 4
BLOCKS = 8
MARGIN = OFFSETS // 2
VMEM_BYTES = 4 << 20

hale_weight = 0.0255
edge_weight = 0.25 - 0.5 * hale_weight
corner_weight = 0.125 + 0.25 * hale_weight
growth = 1.0 / (2.0 * edge_weight)
miller_start = 32

VMEM = pl.BlockSpec(memory_space=pltpu.VMEM)
SMEM = pl.BlockSpec(memory_space=pltpu.SMEM)
HBM = pl.BlockSpec(memory_space=pltpu.HBM)
ANY = pl.BlockSpec(memory_space=pl.ANY)


def call(kernel, outs, in_specs, scratch, args, flops=0, out_specs=None):
    moved = 4 * sum(int(a.size) for a in (*args, *outs))
    return pl.pallas_call(
        kernel,
        out_shape=outs,
        in_specs=in_specs,
        out_specs=out_specs or [VMEM] * len(outs),
        scratch_shapes=scratch,
        compiler_params=pltpu.CompilerParams(vmem_limit_bytes=VMEM_BYTES),
        cost_estimate=pl.CostEstimate(flops=flops, bytes_accessed=moved, transcendentals=0),
    )(*args)


def in_hbm(*arrays):
    return tuple(pltpu.with_memory_space_constraint(x, pltpu.HBM) for x in arrays)


def f32(*shape):
    return jax.ShapeDtypeStruct(shape, jnp.float32)


def table_kernel(phase_hbm, slow_hbm, out_ref, z_ref, phase_ref, slow_ref, sem):
    copies = [
        pltpu.make_async_copy(phase_hbm, phase_ref, sem.at[0]),
        pltpu.make_async_copy(slow_hbm, slow_ref, sem.at[1]),
    ]
    for copy in copies:
        copy.start()
    for copy in copies:
        copy.wait()
    first = lax.axis_size("depth") - 1 - lax.axis_index("depth")
    classes = slow_ref.shape[1]
    z_ref[...] = jnp.full(z_ref.shape, 6.0, jnp.float32)
    for turn in range(TURNS):
        z_ref[turn : turn + 1, 0:classes] = slow_ref[...] * phase_ref[first + turn]
    phases = z_ref[...]
    values = [None] * (miller_start + 1)
    upper = jnp.zeros_like(phases)
    current = jnp.ones_like(phases)
    values[miller_start] = current
    inverse = 1.0 / phases
    for k in range(miller_start, 0, -1):
        lower = (2.0 * k * inverse) * current - upper
        values[k - 1] = lower
        upper, current = current, lower
    evens = values[2]
    for k in range(4, miller_start + 1, 2):
        evens = evens + values[k]
    scale = 1.0 / (values[0] + 2.0 * evens)
    for k in range(TERMS):
        factor = (1.0 if k == 0 else 2.0) * (1.0 if k % 4 < 2 else -1.0) * growth**-k
        ratio = values[k] * scale * factor
        for turn in range(TURNS):
            out_ref[turn, k] = jnp.broadcast_to(ratio[turn : turn + 1, :], (SUBLANES, LANES))


def pick(row, classes):
    dimensions = lax.GatherDimensionNumbers(
        offset_dims=(),
        collapsed_slice_dims=(1,),
        start_index_map=(1,),
        operand_batching_dims=(0,),
        start_indices_batching_dims=(0,),
    )
    return lax.gather(
        row, classes[..., None], dimensions, (1, 1), mode=lax.GatherScatterMode.PROMISE_IN_BOUNDS
    )


def advance(a, b, total, coefficients_of, valid_rows):
    length, tiles = a.shape[1], a.shape[2]
    tile = (SUBLANES, LANES)
    lane = lax.broadcasted_iota(jnp.int32, tile, 1)
    block = lax.broadcasted_iota(jnp.int32, tile, 0)
    after_first, before_last = lane > 0, lane < LANES - 1
    zero = jnp.zeros(tile, jnp.float32)

    def doubled(above, middle, below):
        vertical = [above[h] + below[h] for h in range(tiles)]
        spread = [(corner_weight / edge_weight) * vertical[h] + middle[h] for h in range(tiles)]
        from_left = jnp.where(after_first, pltpu.roll(spread[tiles - 1], 1, 1), zero)
        from_right = jnp.where(before_last, pltpu.roll(spread[0], LANES - 1, 1), zero)
        result = []
        for h in range(tiles):
            left = spread[h - 1] if h else from_left
            right = spread[h + 1] if h + 1 < tiles else from_right
            result.append((left + right) + (vertical[h] - (middle[h] + middle[h])))
        return result

    def sweep(source, target, k, odd, first):
        def row_of(c, i):
            if i < 0:
                return [
                    jnp.where(block == 0, zero, pltpu.roll(source[c, length - 1, h], 1, 0))
                    for h in range(tiles)
                ]
            if i == length:
                return [
                    jnp.where(block == BLOCKS - 1, zero, pltpu.roll(source[c, 0, h], SUBLANES - 1, 0))
                    for h in range(tiles)
                ]
            return [source[c, i, h] for h in range(tiles)]

        coefficient_at = coefficients_of(k, odd)
        if first:
            start_at = coefficients_of(0, False)
        near = [(row_of(c, -1), row_of(c, 0)) for c in range(2)]
        for i in range(length):
            if valid_rows is not None:
                at = block * length + i
                inside = (at >= valid_rows[0]) & (at < valid_rows[1])
            values = []
            for c in range(2):
                above, middle = near[c]
                below = row_of(c, i + 1)
                near[c] = (middle, below)
                result = doubled(above, middle, below)
                for h in range(tiles):
                    value = 0.5 * result[h] if first else result[h] - (growth * growth) * target[c, i, h]
                    if valid_rows is not None:
                        value = jnp.where(inside, value, zero)
                    target[c, i, h] = value
                    result[h] = value
                values.append(result)
            for h in range(tiles):
                coefficient = coefficient_at(i, h)
                if first:
                    start = start_at(i, h)
                    sums = [start * source[c, i, h] for c in range(2)]
                else:
                    sums = [total[c, i, h] for c in range(2)]
                if odd:
                    total[0, i, h] = sums[0] - coefficient * values[1][h]
                    total[1, i, h] = sums[1] + coefficient * values[0][h]
                else:
                    total[0, i, h] = sums[0] + coefficient * values[0][h]
                    total[1, i, h] = sums[1] + coefficient * values[1][h]

    sweep(a, b, 1, True, True)

    def pair(n, carry):
        sweep(b, a, 2 * n, False, False)
        sweep(a, b, 2 * n + 1, True, False)
        return carry

    lax.fori_loop(1, TERMS // 2, pair, 0)


def looked_up(classes, table, turn, side):
    def coefficients_of(k, odd):
        row = table[turn, k]
        if odd:
            row = row * sign_of(side)
        return lambda i, h: pick(row, classes[i, h])

    return coefficients_of


def stored(ref):
    return lambda k, odd: lambda i, h: ref[k, i, h]


def coefficient_kernel(turn, blocks_ref, table_ref, out_ref):
    coefficients_of = looked_up(blocks_ref, table_ref, turn, lax.axis_index("lat"))
    for k in range(TERMS):
        coefficient_at = coefficients_of(k, k % 2 == 1)
        for i in range(out_ref.shape[1]):
            for h in range(out_ref.shape[2]):
                out_ref[k, i, h] = coefficient_at(i, h)


def picked(sources, indices, which):
    result = pick(sources[0], indices)
    for n in range(1, len(sources)):
        result = jnp.where(which == n, pick(sources[n], indices), result)
    return result


def interleaved(tiles_of, rows):
    tiles = len(tiles_of)
    lane = lax.broadcasted_iota(jnp.int32, (rows, LANES), 1)
    return [
        picked(tiles_of, (tiles * lane + j) % LANES, (tiles * lane + j) // LANES) for j in range(tiles)
    ]


def natural_order(tiles_of, rows):
    tiles = len(tiles_of)
    lane = lax.broadcasted_iota(jnp.int32, (rows, LANES), 1)
    return [
        picked(tiles_of, (LANES * t + lane) // tiles, (LANES * t + lane) % tiles) for t in range(tiles)
    ]


def sign_of(side):
    return jnp.where(side == 0, 1.0, -1.0).astype(jnp.float32)


def block_of(natural, c, i, h, length):
    return natural[h, pl.ds(PAD + c * BLOCKS * length + i, BLOCKS, stride=length), :]


def gather_blocks(natural, target):
    length = target.shape[1]
    for c in range(2):
        for i in range(length):
            for h in range(target.shape[2]):
                target[c, i, h] = block_of(natural, c, i, h, length)


PAD = 8


def windows(blocks, natural, own_ref, send_ref):
    side = lax.axis_index("lat")
    _, length, tiles, _, _ = blocks.shape
    rows = BLOCKS * length
    strip_rows = rows // 2
    for c in range(2):
        for i in range(length):
            for h in range(tiles):
                natural[h, pl.ds(PAD + c * rows + i, BLOCKS, stride=length), :] = blocks[c, i, h]
    for ref, strip in ((own_ref, side), (send_ref, 1 - side)):
        if ref is None:
            continue
        begin = strip * strip_rows - MARGIN
        for component in range(2):
            for r in range(0, strip_rows + 2 * MARGIN, SUBLANES):
                at = PAD + component * rows + begin + r
                found = [natural[h, pl.ds(at, SUBLANES), :] for h in range(tiles)]
                row = lax.broadcasted_iota(jnp.int32, (SUBLANES, LANES), 0) + (begin + r)
                inside = (row >= 0) & (row < rows)
                for h, part in enumerate(natural_order(found, SUBLANES)):
                    ref[component, h, r : r + SUBLANES, :] = jnp.where(inside, part, 0.0)


def window_kernel(blocks_ref, *rest):
    *before, own_ref, send_ref, natural = rest
    for ref in before:
        send_ref[: ref.shape[0]] = ref[...]
    windows(blocks_ref, natural, own_ref, send_ref.at[send_ref.shape[0] - 1])


def own_window_kernel(blocks_ref, own_ref, natural):
    windows(blocks_ref, natural, own_ref, None)


def place(natural, source, component, rows, row):
    tiles = natural.shape[0]
    for r in range(0, source.shape[0], SUBLANES):
        parts = [source[r : r + SUBLANES, h * LANES : (h + 1) * LANES] for h in range(tiles)]
        at = pl.multiple_of(PAD + component * rows + row + r, 8)
        for h, part in enumerate(interleaved(parts, SUBLANES)):
            natural[h, pl.ds(at, SUBLANES), :] = part


def split_kernel(in_ref, class_ref, own_ref, send_ref, whole_classes, sem):
    side = lax.axis_index("lat")
    cells = pltpu.make_async_copy(class_ref.at[0], whole_classes, sem.at[0])
    cells.start()
    copies = [
        pltpu.make_async_copy(in_ref.at[0, pl.ds(2 * which, 2)], ref.at[pl.ds(0, 2)], sem.at[j])
        for j, (ref, which) in enumerate(((send_ref, 1 - side), (own_ref, side)), 1)
    ]
    for copy in copies:
        copy.start()
    cells.wait()
    as_float = whole_classes[...].astype(jnp.float32)
    own_ref[2] = as_float
    send_ref[2] = as_float
    for copy in copies:
        copy.wait()


def pack(fields, first, target):
    count = fields.shape[2] // SUBLANES
    for turn in range(TURNS - 1):
        for component in range(2):
            for j in range(count):
                for h in range(target.shape[2]):
                    rows, at = slice(j * SUBLANES, (j + 1) * SUBLANES), slice(h * LANES, (h + 1) * LANES)
                    target[component, turn * count + j, h] = fields[turn, first + component, rows, at]


def unpack(source, turn, natural, component, rows, row):
    tiles = natural.shape[0]
    count = source.shape[1] // (TURNS - 1)
    for j in range(count):
        at = pl.multiple_of(PAD + component * rows + row + j * SUBLANES, 8)
        parts = [source[component, turn * count + j, h] for h in range(tiles)]
        for h, part in enumerate(interleaved(parts, SUBLANES)):
            natural[h, pl.ds(at, SUBLANES), :] = part


def weave_kernel(strips_ref, out_ref):
    tiles = out_ref.shape[1]
    for n in range(strips_ref.shape[0]):
        for r in range(0, strips_ref.shape[1], SUBLANES):
            parts = [
                strips_ref[n, r : r + SUBLANES, h * LANES : (h + 1) * LANES] for h in range(tiles)
            ]
            for h, part in enumerate(interleaved(parts, SUBLANES)):
                out_ref[n, h, r : r + SUBLANES, :] = part


def lay(natural, woven, component, rows, row):
    tiles, count = woven.shape[:2]
    for h in range(tiles):
        at = pl.multiple_of(PAD + component * rows + row, 8)
        natural[h, pl.ds(at, count), :] = woven[h]


def first_kernel(own_ref, got_ref, table_ref, enter_ref, *rest):
    hand_ref, cross_ref, blocks_ref, a, b, natural = rest
    side = lax.axis_index("lat")
    strip_rows = got_ref.shape[1]
    rows = 2 * strip_rows
    length = a.shape[1]
    lay(natural, own_ref[2], 0, rows, side * strip_rows)
    place(natural, got_ref[2], 0, rows, (1 - side) * strip_rows)
    for i in range(length):
        for h in range(a.shape[2]):
            blocks_ref[i, h] = block_of(natural, 0, i, h, length).astype(jnp.int32)
    for component in range(2):
        lay(natural, own_ref[component], component, rows, side * strip_rows)
        place(natural, got_ref[component], component, rows, (1 - side) * strip_rows)
    gather_blocks(natural, a)
    advance(a, b, hand_ref, looked_up(blocks_ref, table_ref, 0, side), None)
    top = lax.axis_index("depth") == 0

    @pl.when(top)
    def _():
        pack(enter_ref, 2 * (1 - side), cross_ref)

    @pl.when(jnp.logical_not(top))
    def _():
        cross_ref[...] = hand_ref[...]


def next_kernel(turn, plane, got_ref, crossed_ref, entered_ref, coefficient_ref, enter_ref, *rest):
    *outs, a, b, natural = rest
    side = lax.axis_index("lat")
    slab = lax.axis_index("depth")
    strip_rows = enter_ref.shape[2]
    rows = 2 * strip_rows

    @pl.when(slab == 0)
    def _():
        for component in range(2):
            place(natural, enter_ref[turn - 1, 2 * side + component], component, rows, side * strip_rows)
            unpack(entered_ref, turn - 1, natural, component, rows, (1 - side) * strip_rows)
        gather_blocks(natural, a)

    @pl.when((slab > 0) & (slab % plane == 0))
    def _():
        a[...] = crossed_ref[...]

    @pl.when(slab % plane > 0)
    def _():
        a[...] = got_ref[...]

    if turn == TURNS - 1:
        advance(a, b, outs[0], stored(coefficient_ref), None)
        windows(outs[0], natural, None, outs[1])
    else:
        advance(a, b, outs[0], stored(coefficient_ref), None)


def correlate(mine, got, strip_rows, images):
    sign = jnp.where(lax.axis_index("lat") == 0, 1, -1)
    tiles = mine[0].shape[1]
    for h in range(tiles):
        for o in range(OFFSETS):
            lag = sign * (o - MARGIN)
            total = None
            for ours, theirs in zip(mine, got):
                for component in range(2):
                    product = (
                        ours[component, h, pl.ds(MARGIN - lag, strip_rows), :]
                        * theirs[component, h, pl.ds(MARGIN + lag, strip_rows), :]
                    )
                    total = product if total is None else total + product
            images(o, h, total)


def early_kernel(*refs):
    *ours, theirs, out_ref = refs

    def images(o, h, total):
        out_ref[o, h] = total

    correlate(ours, [theirs.at[t] for t in range(len(ours))], out_ref.shape[2], images)


def image_kernel(early_ref, mine_ref, got_ref, images_out, wave_out, images_ref, wave_ref, sem):
    side = lax.axis_index("lat")
    strip_rows = wave_ref.shape[1]
    tiles = mine_ref.shape[1]
    rows = slice(MARGIN, MARGIN + strip_rows)
    for ref, which in ((mine_ref, side), (got_ref, 1 - side)):
        for component in range(2):
            for h in range(tiles):
                wave_ref[2 * which + component, :, h * LANES : (h + 1) * LANES] = ref[component, h, rows, :]
    copies = [pltpu.make_async_copy(wave_ref, wave_out.at[0], sem.at[0])]
    copies[0].start()
    done = []

    def images(o, h, total):
        images_ref[h, o] = early_ref[o, h] + total
        done.append(o)
        if len(done) % OFFSETS == 0:
            copy = pltpu.make_async_copy(
                images_ref.at[h], images_out.at[0, :, :, pl.ds(h * LANES, LANES)], sem.at[1 + h]
            )
            copy.start()
            copies.append(copy)

    correlate([mine_ref], [got_ref], strip_rows, images)
    for copy in copies:
        copy.wait()


def field_scratch(length, tiles):
    return [pltpu.VMEM((2, length, tiles, BLOCKS, LANES), jnp.float32)] * 2


def coefficients(freq_phase, class_slowness):
    (table,) = call(
        table_kernel,
        [f32(TURNS, TERMS, SUBLANES, LANES)],
        [HBM, HBM],
        [
            pltpu.VMEM((SUBLANES, LANES), jnp.float32),
            pltpu.SMEM(freq_phase.shape, jnp.float32),
            pltpu.VMEM((1, class_slowness.shape[0]), jnp.float32),
            pltpu.SemaphoreType.DMA((2,)),
        ],
        in_hbm(freq_phase, class_slowness.reshape(1, -1)),
    )
    return table


def paired(in_flight, entering, classes, freq_phase, class_slowness):
    depth = lax.axis_size("depth")
    _, _, strip_rows, width = in_flight.shape
    tiles = width // LANES
    length = 2 * strip_rows // BLOCKS
    swap = [(0, 1), (1, 0)]
    plane = PLANE if depth % PLANE == 0 else depth
    ring = [(i, i - i % plane + (i + 1) % plane) for i in range(depth)]

    def crossing(loops):
        ways = {}
        for loop in loops:
            ways.update(zip(loop, (*loop[1:], loop[0])))
        return [(2 * d + c, 2 * ways[d] + c if d in ways else 2 * d + 1 - c) for d in range(depth) for c in range(2)]

    starts = range(plane, depth, plane)
    loops = [(first - 1, first, first - 3) for first in starts]
    later = [(first - 1, first, first + 2) for first in starts]
    if loops:
        loops.append((depth - 2, depth - 1))
        later += [(0, 1), *((first + 1, first + 1 + plane) for first in starts[:-1:2])]
    cross = {1: crossing(loops), 2: crossing(later)}
    blocks = f32(2, length, tiles, BLOCKS, LANES)
    window = f32(2, tiles, strip_rows + 2 * MARGIN, LANES)
    natural = pltpu.VMEM((tiles, 2 * BLOCKS * length + 2 * PAD, LANES), jnp.float32)
    scratch = field_scratch(length, tiles) + [natural]
    strips = f32(3, strip_rows, width)
    flops = 20 * TERMS * 4 * strip_rows * width

    own, send = call(
        split_kernel,
        [strips, strips],
        [HBM, HBM],
        [pltpu.VMEM((strip_rows, width), jnp.int32), pltpu.SemaphoreType.DMA((3,))],
        in_hbm(in_flight, classes),
    )
    got = lax.ppermute(send, "lat", swap)
    freq_phase, _ = lax.optimization_barrier((freq_phase, own))
    (own,) = call(weave_kernel, [f32(3, tiles, strip_rows, LANES)], [VMEM], [], (own,))
    table = coefficients(freq_phase, class_slowness)
    hand, over, cells = call(
        first_kernel,
        [blocks, blocks, jax.ShapeDtypeStruct(blocks.shape[1:], jnp.int32)],
        [VMEM, VMEM, VMEM, VMEM],
        scratch,
        (own, got, table, entering),
        flops,
    )
    mines, sent, coefficient = [], (), {}
    for turn in range(1, TURNS):
        handed = lax.ppermute(hand, "depth", ring)
        crossed = lax.ppermute(over, ("depth", "lat"), cross[min(turn, 2)])
        if turn == 1:
            entered = crossed
        mine, send = call(
            window_kernel,
            [window, f32(turn, *window.shape)],
            [VMEM] * (1 + len(sent)),
            [natural],
            (hand, *sent),
        )
        mines.append(mine)
        if turn == 1:
            for later in range(1, TURNS):
                (coefficient[later],) = call(
                    functools.partial(coefficient_kernel, later),
                    [f32(TERMS, *blocks.shape[1:])],
                    [VMEM] * 2,
                    [],
                    (cells, table),
                )
            coefficient[1], send, *others = lax.optimization_barrier(
                (coefficient[1], send, *(coefficient[later] for later in range(2, TURNS)))
            )
            coefficient.update(zip(range(2, TURNS), others))
        sent = (send,)
        last = turn == TURNS - 1
        outs = call(
            functools.partial(next_kernel, turn, plane),
            [blocks, window] if last else [blocks],
            [VMEM] * 5,
            scratch,
            (handed, crossed, entered, coefficient[turn], entering),
            flops,
        )
        hand = over = outs[0]
    earlier = lax.ppermute(send, "lat", swap)
    hand, send = outs
    got = lax.ppermute(send, "lat", swap)
    (mine,) = call(own_window_kernel, [window], [VMEM], [natural], (hand,))
    (early,) = call(
        early_kernel,
        [f32(OFFSETS, tiles, strip_rows, LANES)],
        [VMEM] * TURNS,
        [],
        (*mines, earlier),
    )
    return tuple(
        call(
            image_kernel,
            [f32(1, OFFSETS, strip_rows, width), f32(1, 4, strip_rows, width)],
            [VMEM] * 3,
            [
                pltpu.VMEM((tiles, OFFSETS, strip_rows, LANES), jnp.float32),
                pltpu.VMEM((4, strip_rows, width), jnp.float32),
                pltpu.SemaphoreType.DMA((1 + tiles,)),
            ],
            (early, mine, got),
            out_specs=[HBM] * 2,
        )
    )


def inside_kernel(turn, limits_ref, field_ref, blocks_ref, table_ref, out_ref, a, b):
    a[...] = field_ref[...]
    side = lax.axis_index("lat") % 2
    valid = (limits_ref[0], limits_ref[1])
    advance(a, b, out_ref, looked_up(blocks_ref, table_ref, turn, side), valid)


def grouped(in_flight, entering, classes, freq_phase, class_slowness):
    depth, strips = lax.axis_size("depth"), lax.axis_size("lat")
    strip = lax.axis_index("lat")
    side, group = strip % 2, strip // 2
    _, _, strip_rows, width = in_flight.shape
    tiles = width // LANES
    core = 2 * strip_rows
    halo = TERMS - 1 + MARGIN
    while (core + 2 * halo) % BLOCKS:
        halo += 1
    rows = core + 2 * halo
    length = rows // BLOCKS
    swap = [(i, i ^ 1) for i in range(strips)]
    shift = [(i, i + 1) for i in range(depth - 1)]
    blocks = f32(2, length, tiles, BLOCKS, LANES)

    def both_strips(mine, sent):
        got = lax.ppermute(sent, "lat", swap)
        return jnp.where(
            side == 0, jnp.concatenate([mine, got], 1), jnp.concatenate([got, mine], 1)
        )

    def own_components(fields):
        return both_strips(
            lax.dynamic_slice_in_dim(fields, 2 * side, 2, 0),
            lax.dynamic_slice_in_dim(fields, 2 * (1 - side), 2, 0),
        )

    def with_halo(cells):
        above = lax.ppermute(cells[:, core - halo :], "lat", [(i, i + 2) for i in range(strips - 2)])
        below = lax.ppermute(cells[:, :halo], "lat", [(i + 2, i) for i in range(strips - 2)])
        return jnp.concatenate([above, cells, below], 1)

    def to_blocks(cells):
        split = cells.reshape(-1, BLOCKS, length, LANES, tiles)
        return split.transpose(0, 2, 4, 1, 3)

    def to_rows(cells):
        return cells.transpose(0, 3, 1, 4, 2).reshape(2, rows, width)

    def window(cells, which):
        begin = halo - MARGIN + which * strip_rows
        return lax.dynamic_slice_in_dim(cells, begin, strip_rows + 2 * MARGIN, 1)

    cells = to_blocks(with_halo(both_strips(classes, classes)))[0]
    table = coefficients(freq_phase, class_slowness)
    before = group * core - halo
    limits = jnp.stack([jnp.maximum(-before, 0), jnp.minimum(strips * strip_rows - before, rows)])
    field = own_components(in_flight[0])
    images = jnp.zeros((OFFSETS, strip_rows, width), jnp.float32)
    for turn in range(TURNS):
        (advanced,) = call(
            functools.partial(inside_kernel, turn),
            [blocks],
            [SMEM, VMEM, VMEM, VMEM],
            field_scratch(length, tiles),
            (limits.astype(jnp.int32), to_blocks(with_halo(field)), cells, table),
        )
        advanced = to_rows(advanced)
        mine = window(advanced, side)
        got = lax.ppermute(window(advanced, 1 - side), "lat", swap)
        source, receiver = jnp.where(side == 0, mine, got), jnp.where(side == 0, got, mine)
        products = []
        for o in range(OFFSETS):
            lag = o - MARGIN
            first = source[:, MARGIN - lag : MARGIN - lag + strip_rows]
            second = receiver[:, MARGIN + lag : MARGIN + lag + strip_rows]
            products.append(first[0] * second[0] + first[1] * second[1])
        images = images + jnp.stack(products)
        if turn + 1 < TURNS:
            handed = lax.ppermute(advanced[:, halo : halo + core], "depth", shift)
            entered = own_components(entering[turn])
            field = jnp.where(lax.axis_index("depth") == 0, entered, handed)
    own = slice(MARGIN, MARGIN + strip_rows)
    return images[None], jnp.concatenate([source[:, own], receiver[:, own]], 0)[None]


def solution(mesh):
    in_specs = (
        P("depth", None, "lat", None),
        P(None, None, "lat", None),
        P("depth", "lat", None),
        P(),
        P(),
    )
    out_specs = (P("depth", None, "lat", None), P("depth", None, "lat", None))
    pair = mesh.shape["lat"] == 2
    local = paired if pair else grouped
    return jax.shard_map(local, mesh=mesh, in_specs=in_specs, out_specs=out_specs, check_vma=False)
```

```python
import functools

import jax
import jax.numpy as jnp
from jax import lax
from jax.experimental import pallas as pl
from jax.experimental.pallas import tpu as pltpu
from jax.sharding import PartitionSpec as P

TERMS = 16
OFFSETS = 8
TURNS = 3
LANES = 128
SUBLANES = 8
PLANE = 4
BLOCKS = 8
MARGIN = OFFSETS // 2
VMEM_BYTES = 4 << 20

hale_weight = 0.0255
edge_weight = 0.25 - 0.5 * hale_weight
corner_weight = 0.125 + 0.25 * hale_weight
growth = 1.0 / (2.0 * edge_weight)
miller_start = 32

VMEM = pl.BlockSpec(memory_space=pltpu.VMEM)
SMEM = pl.BlockSpec(memory_space=pltpu.SMEM)
HBM = pl.BlockSpec(memory_space=pltpu.HBM)
ANY = pl.BlockSpec(memory_space=pl.ANY)


def call(kernel, outs, in_specs, scratch, args, flops=0, out_specs=None):
    moved = 4 * sum(int(a.size) for a in (*args, *outs))
    return pl.pallas_call(
        kernel,
        out_shape=outs,
        in_specs=in_specs,
        out_specs=out_specs or [VMEM] * len(outs),
        scratch_shapes=scratch,
        compiler_params=pltpu.CompilerParams(vmem_limit_bytes=VMEM_BYTES),
        cost_estimate=pl.CostEstimate(flops=flops, bytes_accessed=moved, transcendentals=0),
    )(*args)


def in_hbm(*arrays):
    return tuple(pltpu.with_memory_space_constraint(x, pltpu.HBM) for x in arrays)


def f32(*shape):
    return jax.ShapeDtypeStruct(shape, jnp.float32)


def table_kernel(phase_hbm, slow_hbm, out_ref, z_ref, phase_ref, slow_ref, sem):
    copies = [
        pltpu.make_async_copy(phase_hbm, phase_ref, sem.at[0]),
        pltpu.make_async_copy(slow_hbm, slow_ref, sem.at[1]),
    ]
    for copy in copies:
        copy.start()
    for copy in copies:
        copy.wait()
    first = lax.axis_size("depth") - 1 - lax.axis_index("depth")
    classes = slow_ref.shape[1]
    z_ref[...] = jnp.full(z_ref.shape, 6.0, jnp.float32)
    for turn in range(TURNS):
        z_ref[turn : turn + 1, 0:classes] = slow_ref[...] * phase_ref[first + turn]
    phases = z_ref[...]
    values = [None] * (miller_start + 1)
    upper = jnp.zeros_like(phases)
    current = jnp.ones_like(phases)
    values[miller_start] = current
    inverse = 1.0 / phases
    for k in range(miller_start, 0, -1):
        lower = (2.0 * k * inverse) * current - upper
        values[k - 1] = lower
        upper, current = current, lower
    evens = values[2]
    for k in range(4, miller_start + 1, 2):
        evens = evens + values[k]
    scale = 1.0 / (values[0] + 2.0 * evens)
    for k in range(TERMS):
        factor = (1.0 if k == 0 else 2.0) * (1.0 if k % 4 < 2 else -1.0) * growth**-k
        ratio = values[k] * scale * factor
        for turn in range(TURNS):
            out_ref[turn, k] = jnp.broadcast_to(ratio[turn : turn + 1, :], (SUBLANES, LANES))


def pick(row, classes):
    dimensions = lax.GatherDimensionNumbers(
        offset_dims=(),
        collapsed_slice_dims=(1,),
        start_index_map=(1,),
        operand_batching_dims=(0,),
        start_indices_batching_dims=(0,),
    )
    return lax.gather(
        row, classes[..., None], dimensions, (1, 1), mode=lax.GatherScatterMode.PROMISE_IN_BOUNDS
    )


def advance(a, b, total, coefficients_of, valid_rows, unrolled=False):
    length, tiles = a.shape[1], a.shape[2]
    tile = (SUBLANES, LANES)
    lane = lax.broadcasted_iota(jnp.int32, tile, 1)
    block = lax.broadcasted_iota(jnp.int32, tile, 0)
    after_first, before_last = lane > 0, lane < LANES - 1
    zero = jnp.zeros(tile, jnp.float32)

    def doubled(above, middle, below):
        vertical = [above[h] + below[h] for h in range(tiles)]
        spread = [(corner_weight / edge_weight) * vertical[h] + middle[h] for h in range(tiles)]
        from_left = jnp.where(after_first, pltpu.roll(spread[tiles - 1], 1, 1), zero)
        from_right = jnp.where(before_last, pltpu.roll(spread[0], LANES - 1, 1), zero)
        result = []
        for h in range(tiles):
            left = spread[h - 1] if h else from_left
            right = spread[h + 1] if h + 1 < tiles else from_right
            result.append((left + right) + (vertical[h] - (middle[h] + middle[h])))
        return result

    def sweep(source, target, k, odd, first):
        def row_of(c, i):
            if i < 0:
                return [
                    jnp.where(block == 0, zero, pltpu.roll(source[c, length - 1, h], 1, 0))
                    for h in range(tiles)
                ]
            if i == length:
                return [
                    jnp.where(block == BLOCKS - 1, zero, pltpu.roll(source[c, 0, h], SUBLANES - 1, 0))
                    for h in range(tiles)
                ]
            return [source[c, i, h] for h in range(tiles)]

        coefficient_at = coefficients_of(k, odd)
        if first:
            start_at = coefficients_of(0, False)
        near = [(row_of(c, -1), row_of(c, 0)) for c in range(2)]
        for i in range(length):
            if valid_rows is not None:
                at = block * length + i
                inside = (at >= valid_rows[0]) & (at < valid_rows[1])
            values = []
            for c in range(2):
                above, middle = near[c]
                below = row_of(c, i + 1)
                near[c] = (middle, below)
                result = doubled(above, middle, below)
                for h in range(tiles):
                    value = 0.5 * result[h] if first else result[h] - (growth * growth) * target[c, i, h]
                    if valid_rows is not None:
                        value = jnp.where(inside, value, zero)
                    target[c, i, h] = value
                    result[h] = value
                values.append(result)
            for h in range(tiles):
                coefficient = coefficient_at(i, h)
                if first:
                    start = start_at(i, h)
                    sums = [start * source[c, i, h] for c in range(2)]
                else:
                    sums = [total[c, i, h] for c in range(2)]
                if odd:
                    total[0, i, h] = sums[0] - coefficient * values[1][h]
                    total[1, i, h] = sums[1] + coefficient * values[0][h]
                else:
                    total[0, i, h] = sums[0] + coefficient * values[0][h]
                    total[1, i, h] = sums[1] + coefficient * values[1][h]

    sweep(a, b, 1, True, True)

    def pair(n, carry):
        sweep(b, a, 2 * n, False, False)
        sweep(a, b, 2 * n + 1, True, False)
        return carry

    if unrolled:
        for n in range(1, TERMS // 2):
            pair(n, 0)
    else:
        lax.fori_loop(1, TERMS // 2, pair, 0)


def looked_up(classes, table, turn, side):
    def coefficients_of(k, odd):
        row = table[turn, k]
        if odd:
            row = row * sign_of(side)
        return lambda i, h: pick(row, classes[i, h])

    return coefficients_of


def stored(ref):
    return lambda k, odd: lambda i, h: ref[k, i, h]


def coefficient_kernel(turn, blocks_ref, table_ref, out_ref):
    coefficients_of = looked_up(blocks_ref, table_ref, turn, lax.axis_index("lat"))
    for k in range(TERMS):
        coefficient_at = coefficients_of(k, k % 2 == 1)
        for i in range(out_ref.shape[1]):
            for h in range(out_ref.shape[2]):
                out_ref[k, i, h] = coefficient_at(i, h)


def picked(sources, indices, which):
    result = pick(sources[0], indices)
    for n in range(1, len(sources)):
        result = jnp.where(which == n, pick(sources[n], indices), result)
    return result


def interleaved(tiles_of, rows):
    tiles = len(tiles_of)
    lane = lax.broadcasted_iota(jnp.int32, (rows, LANES), 1)
    return [
        picked(tiles_of, (tiles * lane + j) % LANES, (tiles * lane + j) // LANES) for j in range(tiles)
    ]


def natural_order(tiles_of, rows):
    tiles = len(tiles_of)
    lane = lax.broadcasted_iota(jnp.int32, (rows, LANES), 1)
    return [
        picked(tiles_of, (LANES * t + lane) // tiles, (LANES * t + lane) % tiles) for t in range(tiles)
    ]


def sign_of(side):
    return jnp.where(side == 0, 1.0, -1.0).astype(jnp.float32)


def block_of(natural, c, i, h, length):
    return natural[h, pl.ds(PAD + c * BLOCKS * length + i, BLOCKS, stride=length), :]


def gather_blocks(natural, target):
    length = target.shape[1]
    for c in range(2):
        for i in range(length):
            for h in range(target.shape[2]):
                target[c, i, h] = block_of(natural, c, i, h, length)


PAD = 8


def windows(blocks, natural, own_ref, send_ref):
    side = lax.axis_index("lat")
    _, length, tiles, _, _ = blocks.shape
    rows = BLOCKS * length
    strip_rows = rows // 2
    for c in range(2):
        for i in range(length):
            for h in range(tiles):
                natural[h, pl.ds(PAD + c * rows + i, BLOCKS, stride=length), :] = blocks[c, i, h]
    for ref, strip in ((own_ref, side), (send_ref, 1 - side)):
        if ref is None:
            continue
        begin = strip * strip_rows - MARGIN
        for component in range(2):
            for r in range(0, strip_rows + 2 * MARGIN, SUBLANES):
                at = PAD + component * rows + begin + r
                found = [natural[h, pl.ds(at, SUBLANES), :] for h in range(tiles)]
                row = lax.broadcasted_iota(jnp.int32, (SUBLANES, LANES), 0) + (begin + r)
                inside = (row >= 0) & (row < rows)
                for h, part in enumerate(natural_order(found, SUBLANES)):
                    ref[component, h, r : r + SUBLANES, :] = jnp.where(inside, part, 0.0)


def window_kernel(blocks_ref, *rest):
    *before, own_ref, send_ref, natural = rest
    for ref in before:
        send_ref[: ref.shape[0]] = ref[...]
    windows(blocks_ref, natural, own_ref, send_ref.at[send_ref.shape[0] - 1])


def own_window_kernel(blocks_ref, own_ref, natural):
    windows(blocks_ref, natural, own_ref, None)


def place(natural, source, component, rows, row):
    tiles = natural.shape[0]
    for r in range(0, source.shape[0], SUBLANES):
        parts = [source[r : r + SUBLANES, h * LANES : (h + 1) * LANES] for h in range(tiles)]
        at = pl.multiple_of(PAD + component * rows + row + r, 8)
        for h, part in enumerate(interleaved(parts, SUBLANES)):
            natural[h, pl.ds(at, SUBLANES), :] = part


def split_kernel(in_ref, class_ref, own_ref, send_ref, whole_classes, sem):
    side = lax.axis_index("lat")
    cells = pltpu.make_async_copy(class_ref.at[0], whole_classes, sem.at[0])
    cells.start()
    copies = [
        pltpu.make_async_copy(in_ref.at[0, pl.ds(2 * which, 2)], ref.at[pl.ds(0, 2)], sem.at[j])
        for j, (ref, which) in enumerate(((send_ref, 1 - side), (own_ref, side)), 1)
    ]
    for copy in copies:
        copy.start()
    cells.wait()
    as_float = whole_classes[...].astype(jnp.float32)
    own_ref[2] = as_float
    send_ref[2] = as_float
    for copy in copies:
        copy.wait()


def pack(fields, first, target):
    count = fields.shape[2] // SUBLANES
    for turn in range(TURNS - 1):
        for component in range(2):
            for j in range(count):
                for h in range(target.shape[2]):
                    rows, at = slice(j * SUBLANES, (j + 1) * SUBLANES), slice(h * LANES, (h + 1) * LANES)
                    target[component, turn * count + j, h] = fields[turn, first + component, rows, at]


def unpack(source, turn, natural, component, rows, row):
    tiles = natural.shape[0]
    count = source.shape[1] // (TURNS - 1)
    for j in range(count):
        at = pl.multiple_of(PAD + component * rows + row + j * SUBLANES, 8)
        parts = [source[component, turn * count + j, h] for h in range(tiles)]
        for h, part in enumerate(interleaved(parts, SUBLANES)):
            natural[h, pl.ds(at, SUBLANES), :] = part


def weave_kernel(strips_ref, out_ref):
    tiles = out_ref.shape[1]
    for n in range(strips_ref.shape[0]):
        for r in range(0, strips_ref.shape[1], SUBLANES):
            parts = [
                strips_ref[n, r : r + SUBLANES, h * LANES : (h + 1) * LANES] for h in range(tiles)
            ]
            for h, part in enumerate(interleaved(parts, SUBLANES)):
                out_ref[n, h, r : r + SUBLANES, :] = part


def lay(natural, woven, component, rows, row):
    tiles, count = woven.shape[:2]
    for h in range(tiles):
        at = pl.multiple_of(PAD + component * rows + row, 8)
        natural[h, pl.ds(at, count), :] = woven[h]


def first_kernel(own_ref, got_ref, table_ref, enter_ref, *rest):
    hand_ref, cross_ref, blocks_ref, a, b, natural = rest
    side = lax.axis_index("lat")
    strip_rows = got_ref.shape[1]
    rows = 2 * strip_rows
    length = a.shape[1]
    lay(natural, own_ref[2], 0, rows, side * strip_rows)
    place(natural, got_ref[2], 0, rows, (1 - side) * strip_rows)
    for i in range(length):
        for h in range(a.shape[2]):
            blocks_ref[i, h] = block_of(natural, 0, i, h, length).astype(jnp.int32)
    for component in range(2):
        lay(natural, own_ref[component], component, rows, side * strip_rows)
        place(natural, got_ref[component], component, rows, (1 - side) * strip_rows)
    gather_blocks(natural, a)
    advance(a, b, hand_ref, looked_up(blocks_ref, table_ref, 0, side), None, unrolled=True)
    top = lax.axis_index("depth") == 0

    @pl.when(top)
    def _():
        pack(enter_ref, 2 * (1 - side), cross_ref)

    @pl.when(jnp.logical_not(top))
    def _():
        cross_ref[...] = hand_ref[...]


def next_kernel(turn, plane, got_ref, crossed_ref, entered_ref, coefficient_ref, enter_ref, *rest):
    *outs, a, b, natural = rest
    side = lax.axis_index("lat")
    slab = lax.axis_index("depth")
    strip_rows = enter_ref.shape[2]
    rows = 2 * strip_rows

    @pl.when(slab == 0)
    def _():
        for component in range(2):
            place(natural, enter_ref[turn - 1, 2 * side + component], component, rows, side * strip_rows)
            unpack(entered_ref, turn - 1, natural, component, rows, (1 - side) * strip_rows)
        gather_blocks(natural, a)

    @pl.when((slab > 0) & (slab % plane == 0))
    def _():
        a[...] = crossed_ref[...]

    @pl.when(slab % plane > 0)
    def _():
        a[...] = got_ref[...]

    if turn == TURNS - 1:
        advance(a, b, outs[0], stored(coefficient_ref), None)
        windows(outs[0], natural, None, outs[1])
    else:
        advance(a, b, outs[0], stored(coefficient_ref), None)


def correlate(mine, got, strip_rows, images):
    sign = jnp.where(lax.axis_index("lat") == 0, 1, -1)
    tiles = mine[0].shape[1]
    for h in range(tiles):
        for o in range(OFFSETS):
            lag = sign * (o - MARGIN)
            total = None
            for ours, theirs in zip(mine, got):
                for component in range(2):
                    product = (
                        ours[component, h, pl.ds(MARGIN - lag, strip_rows), :]
                        * theirs[component, h, pl.ds(MARGIN + lag, strip_rows), :]
                    )
                    total = product if total is None else total + product
            images(o, h, total)


def early_kernel(*refs):
    *ours, theirs, out_ref = refs

    def images(o, h, total):
        out_ref[o, h] = total

    correlate(ours, [theirs.at[t] for t in range(len(ours))], out_ref.shape[2], images)


def image_kernel(early_ref, mine_ref, got_ref, images_out, wave_out, images_ref, wave_ref, sem):
    side = lax.axis_index("lat")
    strip_rows = wave_ref.shape[1]
    tiles = mine_ref.shape[1]
    rows = slice(MARGIN, MARGIN + strip_rows)
    for ref, which in ((mine_ref, side), (got_ref, 1 - side)):
        for component in range(2):
            for h in range(tiles):
                wave_ref[2 * which + component, :, h * LANES : (h + 1) * LANES] = ref[component, h, rows, :]
    copies = [pltpu.make_async_copy(wave_ref, wave_out.at[0], sem.at[0])]
    copies[0].start()
    done = []

    def images(o, h, total):
        images_ref[h, o] = early_ref[o, h] + total
        done.append(o)
        if len(done) % OFFSETS == 0:
            copy = pltpu.make_async_copy(
                images_ref.at[h], images_out.at[0, :, :, pl.ds(h * LANES, LANES)], sem.at[1 + h]
            )
            copy.start()
            copies.append(copy)

    correlate([mine_ref], [got_ref], strip_rows, images)
    for copy in copies:
        copy.wait()


def field_scratch(length, tiles):
    return [pltpu.VMEM((2, length, tiles, BLOCKS, LANES), jnp.float32)] * 2


def coefficients(freq_phase, class_slowness):
    (table,) = call(
        table_kernel,
        [f32(TURNS, TERMS, SUBLANES, LANES)],
        [HBM, HBM],
        [
            pltpu.VMEM((SUBLANES, LANES), jnp.float32),
            pltpu.SMEM(freq_phase.shape, jnp.float32),
            pltpu.VMEM((1, class_slowness.shape[0]), jnp.float32),
            pltpu.SemaphoreType.DMA((2,)),
        ],
        in_hbm(freq_phase, class_slowness.reshape(1, -1)),
    )
    return table


def paired(in_flight, entering, classes, freq_phase, class_slowness):
    depth = lax.axis_size("depth")
    _, _, strip_rows, width = in_flight.shape
    tiles = width // LANES
    length = 2 * strip_rows // BLOCKS
    swap = [(0, 1), (1, 0)]
    plane = PLANE if depth % PLANE == 0 else depth
    ring = [(i, i - i % plane + (i + 1) % plane) for i in range(depth)]

    def crossing(loops):
        ways = {}
        for loop in loops:
            ways.update(zip(loop, (*loop[1:], loop[0])))
        return [(2 * d + c, 2 * ways[d] + c if d in ways else 2 * d + 1 - c) for d in range(depth) for c in range(2)]

    starts = range(plane, depth, plane)
    loops = [(first - 1, first, first - 3) for first in starts]
    later = [(first - 1, first, first + 2) for first in starts]
    if loops:
        loops.append((depth - 2, depth - 1))
        later += [(0, 1), *((first + 1, first + 1 + plane) for first in starts[:-1:2])]
    cross = {1: crossing(loops), 2: crossing(later)}
    blocks = f32(2, length, tiles, BLOCKS, LANES)
    window = f32(2, tiles, strip_rows + 2 * MARGIN, LANES)
    natural = pltpu.VMEM((tiles, 2 * BLOCKS * length + 2 * PAD, LANES), jnp.float32)
    scratch = field_scratch(length, tiles) + [natural]
    strips = f32(3, strip_rows, width)
    flops = 20 * TERMS * 4 * strip_rows * width

    own, send = call(
        split_kernel,
        [strips, strips],
        [HBM, HBM],
        [pltpu.VMEM((strip_rows, width), jnp.int32), pltpu.SemaphoreType.DMA((3,))],
        in_hbm(in_flight, classes),
    )
    got = lax.ppermute(send, "lat", swap)
    freq_phase, _ = lax.optimization_barrier((freq_phase, own))
    (own,) = call(weave_kernel, [f32(3, tiles, strip_rows, LANES)], [VMEM], [], (own,))
    table = coefficients(freq_phase, class_slowness)
    hand, over, cells = call(
        first_kernel,
        [blocks, blocks, jax.ShapeDtypeStruct(blocks.shape[1:], jnp.int32)],
        [VMEM, VMEM, VMEM, VMEM],
        scratch,
        (own, got, table, entering),
        flops,
    )
    mines, sent, coefficient = [], (), {}
    for turn in range(1, TURNS):
        handed = lax.ppermute(hand, "depth", ring)
        crossed = lax.ppermute(over, ("depth", "lat"), cross[min(turn, 2)])
        if turn == 1:
            entered = crossed
        mine, send = call(
            window_kernel,
            [window, f32(turn, *window.shape)],
            [VMEM] * (1 + len(sent)),
            [natural],
            (hand, *sent),
        )
        mines.append(mine)
        if turn == 1:
            for later in range(1, TURNS):
                (coefficient[later],) = call(
                    functools.partial(coefficient_kernel, later),
                    [f32(TERMS, *blocks.shape[1:])],
                    [VMEM] * 2,
                    [],
                    (cells, table),
                )
            coefficient[1], send, *others = lax.optimization_barrier(
                (coefficient[1], send, *(coefficient[later] for later in range(2, TURNS)))
            )
            coefficient.update(zip(range(2, TURNS), others))
        sent = (send,)
        last = turn == TURNS - 1
        outs = call(
            functools.partial(next_kernel, turn, plane),
            [blocks, window] if last else [blocks],
            [VMEM] * 5,
            scratch,
            (handed, crossed, entered, coefficient[turn], entering),
            flops,
        )
        hand = over = outs[0]
    earlier = lax.ppermute(send, "lat", swap)
    hand, send = outs
    got = lax.ppermute(send, "lat", swap)
    (mine,) = call(own_window_kernel, [window], [VMEM], [natural], (hand,))
    (early,) = call(
        early_kernel,
        [f32(OFFSETS, tiles, strip_rows, LANES)],
        [VMEM] * TURNS,
        [],
        (*mines, earlier),
    )
    return tuple(
        call(
            image_kernel,
            [f32(1, OFFSETS, strip_rows, width), f32(1, 4, strip_rows, width)],
            [VMEM] * 3,
            [
                pltpu.VMEM((tiles, OFFSETS, strip_rows, LANES), jnp.float32),
                pltpu.VMEM((4, strip_rows, width), jnp.float32),
                pltpu.SemaphoreType.DMA((1 + tiles,)),
            ],
            (early, mine, got),
            out_specs=[HBM] * 2,
        )
    )


def inside_kernel(turn, limits_ref, field_ref, blocks_ref, table_ref, out_ref, a, b):
    a[...] = field_ref[...]
    side = lax.axis_index("lat") % 2
    valid = (limits_ref[0], limits_ref[1])
    advance(a, b, out_ref, looked_up(blocks_ref, table_ref, turn, side), valid)


def grouped(in_flight, entering, classes, freq_phase, class_slowness):
    depth, strips = lax.axis_size("depth"), lax.axis_size("lat")
    strip = lax.axis_index("lat")
    side, group = strip % 2, strip // 2
    _, _, strip_rows, width = in_flight.shape
    tiles = width // LANES
    core = 2 * strip_rows
    halo = TERMS - 1 + MARGIN
    while (core + 2 * halo) % BLOCKS:
        halo += 1
    rows = core + 2 * halo
    length = rows // BLOCKS
    swap = [(i, i ^ 1) for i in range(strips)]
    shift = [(i, i + 1) for i in range(depth - 1)]
    blocks = f32(2, length, tiles, BLOCKS, LANES)

    def both_strips(mine, sent):
        got = lax.ppermute(sent, "lat", swap)
        return jnp.where(
            side == 0, jnp.concatenate([mine, got], 1), jnp.concatenate([got, mine], 1)
        )

    def own_components(fields):
        return both_strips(
            lax.dynamic_slice_in_dim(fields, 2 * side, 2, 0),
            lax.dynamic_slice_in_dim(fields, 2 * (1 - side), 2, 0),
        )

    def with_halo(cells):
        above = lax.ppermute(cells[:, core - halo :], "lat", [(i, i + 2) for i in range(strips - 2)])
        below = lax.ppermute(cells[:, :halo], "lat", [(i + 2, i) for i in range(strips - 2)])
        return jnp.concatenate([above, cells, below], 1)

    def to_blocks(cells):
        split = cells.reshape(-1, BLOCKS, length, LANES, tiles)
        return split.transpose(0, 2, 4, 1, 3)

    def to_rows(cells):
        return cells.transpose(0, 3, 1, 4, 2).reshape(2, rows, width)

    def window(cells, which):
        begin = halo - MARGIN + which * strip_rows
        return lax.dynamic_slice_in_dim(cells, begin, strip_rows + 2 * MARGIN, 1)

    cells = to_blocks(with_halo(both_strips(classes, classes)))[0]
    table = coefficients(freq_phase, class_slowness)
    before = group * core - halo
    limits = jnp.stack([jnp.maximum(-before, 0), jnp.minimum(strips * strip_rows - before, rows)])
    field = own_components(in_flight[0])
    images = jnp.zeros((OFFSETS, strip_rows, width), jnp.float32)
    for turn in range(TURNS):
        (advanced,) = call(
            functools.partial(inside_kernel, turn),
            [blocks],
            [SMEM, VMEM, VMEM, VMEM],
            field_scratch(length, tiles),
            (limits.astype(jnp.int32), to_blocks(with_halo(field)), cells, table),
        )
        advanced = to_rows(advanced)
        mine = window(advanced, side)
        got = lax.ppermute(window(advanced, 1 - side), "lat", swap)
        source, receiver = jnp.where(side == 0, mine, got), jnp.where(side == 0, got, mine)
        products = []
        for o in range(OFFSETS):
            lag = o - MARGIN
            first = source[:, MARGIN - lag : MARGIN - lag + strip_rows]
            second = receiver[:, MARGIN + lag : MARGIN + lag + strip_rows]
            products.append(first[0] * second[0] + first[1] * second[1])
        images = images + jnp.stack(products)
        if turn + 1 < TURNS:
            handed = lax.ppermute(advanced[:, halo : halo + core], "depth", shift)
            entered = own_components(entering[turn])
            field = jnp.where(lax.axis_index("depth") == 0, entered, handed)
    own = slice(MARGIN, MARGIN + strip_rows)
    return images[None], jnp.concatenate([source[:, own], receiver[:, own]], 0)[None]


def solution(mesh):
    in_specs = (
        P("depth", None, "lat", None),
        P(None, None, "lat", None),
        P("depth", "lat", None),
        P(),
        P(),
    )
    out_specs = (P("depth", None, "lat", None), P("depth", None, "lat", None))
    pair = mesh.shape["lat"] == 2
    local = paired if pair else grouped
    return jax.shard_map(local, mesh=mesh, in_specs=in_specs, out_specs=out_specs, check_vma=False)
```

```python
import functools

import jax
import jax.numpy as jnp
from jax import lax
from jax.experimental import pallas as pl
from jax.experimental.pallas import tpu as pltpu
from jax.sharding import PartitionSpec as P

TERMS = 16
OFFSETS = 8
TURNS = 3
LANES = 128
SUBLANES = 8
PLANE = 4
BLOCKS = 8
MARGIN = OFFSETS // 2
VMEM_BYTES = 4 << 20

hale_weight = 0.0255
edge_weight = 0.25 - 0.5 * hale_weight
corner_weight = 0.125 + 0.25 * hale_weight
growth = 1.0 / (2.0 * edge_weight)
miller_start = 32

VMEM = pl.BlockSpec(memory_space=pltpu.VMEM)
SMEM = pl.BlockSpec(memory_space=pltpu.SMEM)
HBM = pl.BlockSpec(memory_space=pltpu.HBM)
ANY = pl.BlockSpec(memory_space=pl.ANY)


def call(kernel, outs, in_specs, scratch, args, flops=0, out_specs=None):
    moved = 4 * sum(int(a.size) for a in (*args, *outs))
    return pl.pallas_call(
        kernel,
        out_shape=outs,
        in_specs=in_specs,
        out_specs=out_specs or [VMEM] * len(outs),
        scratch_shapes=scratch,
        compiler_params=pltpu.CompilerParams(vmem_limit_bytes=VMEM_BYTES),
        cost_estimate=pl.CostEstimate(flops=flops, bytes_accessed=moved, transcendentals=0),
    )(*args)


def in_hbm(*arrays):
    return tuple(pltpu.with_memory_space_constraint(x, pltpu.HBM) for x in arrays)


def f32(*shape):
    return jax.ShapeDtypeStruct(shape, jnp.float32)


def table_kernel(phase_hbm, slow_hbm, out_ref, z_ref, phase_ref, slow_ref, sem):
    copies = [
        pltpu.make_async_copy(phase_hbm, phase_ref, sem.at[0]),
        pltpu.make_async_copy(slow_hbm, slow_ref, sem.at[1]),
    ]
    for copy in copies:
        copy.start()
    for copy in copies:
        copy.wait()
    first = lax.axis_size("depth") - 1 - lax.axis_index("depth")
    classes = slow_ref.shape[1]
    z_ref[...] = jnp.full(z_ref.shape, 6.0, jnp.float32)
    for turn in range(TURNS):
        z_ref[turn : turn + 1, 0:classes] = slow_ref[...] * phase_ref[first + turn]
    phases = z_ref[...]
    values = [None] * (miller_start + 1)
    upper = jnp.zeros_like(phases)
    current = jnp.ones_like(phases)
    values[miller_start] = current
    inverse = 1.0 / phases
    for k in range(miller_start, 0, -1):
        lower = (2.0 * k * inverse) * current - upper
        values[k - 1] = lower
        upper, current = current, lower
    evens = values[2]
    for k in range(4, miller_start + 1, 2):
        evens = evens + values[k]
    scale = 1.0 / (values[0] + 2.0 * evens)
    for k in range(TERMS):
        factor = (1.0 if k == 0 else 2.0) * (1.0 if k % 4 < 2 else -1.0) * growth**-k
        ratio = values[k] * scale * factor
        for turn in range(TURNS):
            out_ref[turn, k] = jnp.broadcast_to(ratio[turn : turn + 1, :], (SUBLANES, LANES))


def pick(row, classes):
    dimensions = lax.GatherDimensionNumbers(
        offset_dims=(),
        collapsed_slice_dims=(1,),
        start_index_map=(1,),
        operand_batching_dims=(0,),
        start_indices_batching_dims=(0,),
    )
    return lax.gather(
        row, classes[..., None], dimensions, (1, 1), mode=lax.GatherScatterMode.PROMISE_IN_BOUNDS
    )


def advance(a, b, total, coefficients_of, valid_rows, unrolled=False):
    length, tiles = a.shape[1], a.shape[2]
    tile = (SUBLANES, LANES)
    lane = lax.broadcasted_iota(jnp.int32, tile, 1)
    block = lax.broadcasted_iota(jnp.int32, tile, 0)
    after_first, before_last = lane > 0, lane < LANES - 1
    zero = jnp.zeros(tile, jnp.float32)

    def doubled(above, middle, below):
        vertical = [above[h] + below[h] for h in range(tiles)]
        spread = [(corner_weight / edge_weight) * vertical[h] + middle[h] for h in range(tiles)]
        from_left = jnp.where(after_first, pltpu.roll(spread[tiles - 1], 1, 1), zero)
        from_right = jnp.where(before_last, pltpu.roll(spread[0], LANES - 1, 1), zero)
        result = []
        for h in range(tiles):
            left = spread[h - 1] if h else from_left
            right = spread[h + 1] if h + 1 < tiles else from_right
            result.append((left + right) + (vertical[h] - (middle[h] + middle[h])))
        return result

    def sweep(source, target, k, odd, first):
        def row_of(c, i):
            if i < 0:
                return [
                    jnp.where(block == 0, zero, pltpu.roll(source[c, length - 1, h], 1, 0))
                    for h in range(tiles)
                ]
            if i == length:
                return [
                    jnp.where(block == BLOCKS - 1, zero, pltpu.roll(source[c, 0, h], SUBLANES - 1, 0))
                    for h in range(tiles)
                ]
            return [source[c, i, h] for h in range(tiles)]

        coefficient_at = coefficients_of(k, odd)
        if first:
            start_at = coefficients_of(0, False)
        near = [(row_of(c, -1), row_of(c, 0)) for c in range(2)]
        for i in range(length):
            if valid_rows is not None:
                at = block * length + i
                inside = (at >= valid_rows[0]) & (at < valid_rows[1])
            values = []
            for c in range(2):
                above, middle = near[c]
                below = row_of(c, i + 1)
                near[c] = (middle, below)
                result = doubled(above, middle, below)
                for h in range(tiles):
                    value = 0.5 * result[h] if first else result[h] - (growth * growth) * target[c, i, h]
                    if valid_rows is not None:
                        value = jnp.where(inside, value, zero)
                    target[c, i, h] = value
                    result[h] = value
                values.append(result)
            for h in range(tiles):
                coefficient = coefficient_at(i, h)
                if first:
                    start = start_at(i, h)
                    sums = [start * source[c, i, h] for c in range(2)]
                else:
                    sums = [total[c, i, h] for c in range(2)]
                if odd:
                    total[0, i, h] = sums[0] - coefficient * values[1][h]
                    total[1, i, h] = sums[1] + coefficient * values[0][h]
                else:
                    total[0, i, h] = sums[0] + coefficient * values[0][h]
                    total[1, i, h] = sums[1] + coefficient * values[1][h]

    sweep(a, b, 1, True, True)

    def pair(n, carry):
        sweep(b, a, 2 * n, False, False)
        sweep(a, b, 2 * n + 1, True, False)
        return carry

    if unrolled:
        for n in range(1, TERMS // 2):
            pair(n, 0)
    else:
        pair(1, 0)
        lax.fori_loop(1, TERMS // 4, lambda n, carry: pair(2 * n + 1, pair(2 * n, carry)), 0)


def looked_up(classes, table, turn, side):
    def coefficients_of(k, odd):
        row = table[turn, k]
        if odd:
            row = row * sign_of(side)
        return lambda i, h: pick(row, classes[i, h])

    return coefficients_of


def stored(ref):
    return lambda k, odd: lambda i, h: ref[k, i, h]


def coefficient_kernel(turn, blocks_ref, table_ref, out_ref):
    coefficients_of = looked_up(blocks_ref, table_ref, turn, lax.axis_index("lat"))
    for k in range(TERMS):
        coefficient_at = coefficients_of(k, k % 2 == 1)
        for i in range(out_ref.shape[1]):
            for h in range(out_ref.shape[2]):
                out_ref[k, i, h] = coefficient_at(i, h)


def picked(sources, indices, which):
    result = pick(sources[0], indices)
    for n in range(1, len(sources)):
        result = jnp.where(which == n, pick(sources[n], indices), result)
    return result


def interleaved(tiles_of, rows):
    tiles = len(tiles_of)
    lane = lax.broadcasted_iota(jnp.int32, (rows, LANES), 1)
    return [
        picked(tiles_of, (tiles * lane + j) % LANES, (tiles * lane + j) // LANES) for j in range(tiles)
    ]


def natural_order(tiles_of, rows):
    tiles = len(tiles_of)
    lane = lax.broadcasted_iota(jnp.int32, (rows, LANES), 1)
    return [
        picked(tiles_of, (LANES * t + lane) // tiles, (LANES * t + lane) % tiles) for t in range(tiles)
    ]


def sign_of(side):
    return jnp.where(side == 0, 1.0, -1.0).astype(jnp.float32)


def block_of(natural, c, i, h, length):
    return natural[h, pl.ds(PAD + c * BLOCKS * length + i, BLOCKS, stride=length), :]


def gather_blocks(natural, target):
    length = target.shape[1]
    for c in range(2):
        for i in range(length):
            for h in range(target.shape[2]):
                target[c, i, h] = block_of(natural, c, i, h, length)


PAD = 8


def windows(blocks, natural, own_ref, send_ref):
    side = lax.axis_index("lat")
    _, length, tiles, _, _ = blocks.shape
    rows = BLOCKS * length
    strip_rows = rows // 2
    for c in range(2):
        for i in range(length):
            for h in range(tiles):
                natural[h, pl.ds(PAD + c * rows + i, BLOCKS, stride=length), :] = blocks[c, i, h]
    for ref, strip in ((own_ref, side), (send_ref, 1 - side)):
        if ref is None:
            continue
        begin = strip * strip_rows - MARGIN
        for component in range(2):
            for r in range(0, strip_rows + 2 * MARGIN, SUBLANES):
                at = PAD + component * rows + begin + r
                found = [natural[h, pl.ds(at, SUBLANES), :] for h in range(tiles)]
                row = lax.broadcasted_iota(jnp.int32, (SUBLANES, LANES), 0) + (begin + r)
                inside = (row >= 0) & (row < rows)
                for h, part in enumerate(natural_order(found, SUBLANES)):
                    ref[component, h, r : r + SUBLANES, :] = jnp.where(inside, part, 0.0)


def window_kernel(blocks_ref, *rest):
    *before, own_ref, send_ref, natural = rest
    for ref in before:
        send_ref[: ref.shape[0]] = ref[...]
    windows(blocks_ref, natural, own_ref, send_ref.at[send_ref.shape[0] - 1])


def own_window_kernel(blocks_ref, own_ref, natural):
    windows(blocks_ref, natural, own_ref, None)


def place(natural, source, component, rows, row):
    tiles = natural.shape[0]
    for r in range(0, source.shape[0], SUBLANES):
        parts = [source[r : r + SUBLANES, h * LANES : (h + 1) * LANES] for h in range(tiles)]
        at = pl.multiple_of(PAD + component * rows + row + r, 8)
        for h, part in enumerate(interleaved(parts, SUBLANES)):
            natural[h, pl.ds(at, SUBLANES), :] = part


def strips_of(in_ref, class_ref, which, target, whole_classes, sem):
    cells = pltpu.make_async_copy(class_ref.at[0], whole_classes, sem.at[0])
    fields = pltpu.make_async_copy(in_ref.at[0, pl.ds(2 * which, 2)], target.at[pl.ds(0, 2)], sem.at[1])
    cells.start()
    fields.start()
    cells.wait()
    target[2] = whole_classes[...].astype(jnp.float32)
    fields.wait()


def split_kernel(in_ref, class_ref, send_ref, whole_classes, sem):
    strips_of(in_ref, class_ref, 1 - lax.axis_index("lat"), send_ref, whole_classes, sem)


def pack(fields, first, target):
    count = fields.shape[2] // SUBLANES
    for turn in range(TURNS - 1):
        for component in range(2):
            for j in range(count):
                for h in range(target.shape[2]):
                    rows, at = slice(j * SUBLANES, (j + 1) * SUBLANES), slice(h * LANES, (h + 1) * LANES)
                    target[component, turn * count + j, h] = fields[turn, first + component, rows, at]


def unpack(source, turn, natural, component, rows, row):
    tiles = natural.shape[0]
    count = source.shape[1] // (TURNS - 1)
    for j in range(count):
        at = pl.multiple_of(PAD + component * rows + row + j * SUBLANES, 8)
        parts = [source[component, turn * count + j, h] for h in range(tiles)]
        for h, part in enumerate(interleaved(parts, SUBLANES)):
            natural[h, pl.ds(at, SUBLANES), :] = part


def weave_kernel(in_ref, class_ref, out_ref, strips_ref, whole_classes, sem):
    strips_of(in_ref, class_ref, lax.axis_index("lat"), strips_ref, whole_classes, sem)
    tiles = out_ref.shape[1]
    for n in range(strips_ref.shape[0]):
        for r in range(0, strips_ref.shape[1], SUBLANES):
            parts = [
                strips_ref[n, r : r + SUBLANES, h * LANES : (h + 1) * LANES] for h in range(tiles)
            ]
            for h, part in enumerate(interleaved(parts, SUBLANES)):
                out_ref[n, h, r : r + SUBLANES, :] = part


def lay(natural, woven, component, rows, row):
    tiles, count = woven.shape[:2]
    for h in range(tiles):
        at = pl.multiple_of(PAD + component * rows + row, 8)
        natural[h, pl.ds(at, count), :] = woven[h]


def first_kernel(own_ref, got_ref, table_ref, enter_ref, *rest):
    hand_ref, cross_ref, blocks_ref, a, b, natural = rest
    side = lax.axis_index("lat")
    strip_rows = got_ref.shape[1]
    rows = 2 * strip_rows
    length = a.shape[1]
    lay(natural, own_ref[2], 0, rows, side * strip_rows)
    place(natural, got_ref[2], 0, rows, (1 - side) * strip_rows)
    for i in range(length):
        for h in range(a.shape[2]):
            blocks_ref[i, h] = block_of(natural, 0, i, h, length).astype(jnp.int32)
    for component in range(2):
        lay(natural, own_ref[component], component, rows, side * strip_rows)
        place(natural, got_ref[component], component, rows, (1 - side) * strip_rows)
    gather_blocks(natural, a)
    advance(a, b, hand_ref, looked_up(blocks_ref, table_ref, 0, side), None, unrolled=True)
    top = lax.axis_index("depth") == 0

    @pl.when(top)
    def _():
        pack(enter_ref, 2 * (1 - side), cross_ref)

    @pl.when(jnp.logical_not(top))
    def _():
        cross_ref[...] = hand_ref[...]


def next_kernel(turn, plane, got_ref, crossed_ref, entered_ref, coefficient_ref, enter_ref, *rest):
    *outs, a, b, natural = rest
    side = lax.axis_index("lat")
    slab = lax.axis_index("depth")
    strip_rows = enter_ref.shape[2]
    rows = 2 * strip_rows

    @pl.when(slab == 0)
    def _():
        for component in range(2):
            place(natural, enter_ref[turn - 1, 2 * side + component], component, rows, side * strip_rows)
            unpack(entered_ref, turn - 1, natural, component, rows, (1 - side) * strip_rows)
        gather_blocks(natural, a)

    @pl.when((slab > 0) & (slab % plane == 0))
    def _():
        a[...] = crossed_ref[...]

    @pl.when(slab % plane > 0)
    def _():
        a[...] = got_ref[...]

    if turn == TURNS - 1:
        advance(a, b, outs[0], stored(coefficient_ref), None)
        windows(outs[0], natural, None, outs[1])
    else:
        advance(a, b, outs[0], stored(coefficient_ref), None)


def correlate(mine, got, strip_rows, images):
    sign = jnp.where(lax.axis_index("lat") == 0, 1, -1)
    tiles = mine[0].shape[1]
    for h in range(tiles):
        for o in range(OFFSETS):
            lag = sign * (o - MARGIN)
            total = None
            for ours, theirs in zip(mine, got):
                for component in range(2):
                    product = (
                        ours[component, h, pl.ds(MARGIN - lag, strip_rows), :]
                        * theirs[component, h, pl.ds(MARGIN + lag, strip_rows), :]
                    )
                    total = product if total is None else total + product
            images(o, h, total)


def early_kernel(*refs):
    *ours, theirs, out_ref = refs

    def images(o, h, total):
        out_ref[o, h] = total

    correlate(ours, [theirs.at[t] for t in range(len(ours))], out_ref.shape[2], images)


def image_kernel(early_ref, mine_ref, got_ref, images_out, wave_out, images_ref, wave_ref, sem):
    side = lax.axis_index("lat")
    strip_rows = wave_ref.shape[1]
    tiles = mine_ref.shape[1]
    rows = slice(MARGIN, MARGIN + strip_rows)
    for ref, which in ((mine_ref, side), (got_ref, 1 - side)):
        for component in range(2):
            for h in range(tiles):
                wave_ref[2 * which + component, :, h * LANES : (h + 1) * LANES] = ref[component, h, rows, :]
    copies = [pltpu.make_async_copy(wave_ref, wave_out.at[0], sem.at[0])]
    copies[0].start()
    done = []

    def images(o, h, total):
        images_ref[h, o] = early_ref[o, h] + total
        done.append(o)
        if len(done) % OFFSETS == 0:
            copy = pltpu.make_async_copy(
                images_ref.at[h], images_out.at[0, :, :, pl.ds(h * LANES, LANES)], sem.at[1 + h]
            )
            copy.start()
            copies.append(copy)

    correlate([mine_ref], [got_ref], strip_rows, images)
    for copy in copies:
        copy.wait()


def field_scratch(length, tiles):
    return [pltpu.VMEM((2, length, tiles, BLOCKS, LANES), jnp.float32)] * 2


def coefficients(freq_phase, class_slowness):
    (table,) = call(
        table_kernel,
        [f32(TURNS, TERMS, SUBLANES, LANES)],
        [HBM, HBM],
        [
            pltpu.VMEM((SUBLANES, LANES), jnp.float32),
            pltpu.SMEM(freq_phase.shape, jnp.float32),
            pltpu.VMEM((1, class_slowness.shape[0]), jnp.float32),
            pltpu.SemaphoreType.DMA((2,)),
        ],
        in_hbm(freq_phase, class_slowness.reshape(1, -1)),
    )
    return table


def paired(in_flight, entering, classes, freq_phase, class_slowness):
    depth = lax.axis_size("depth")
    _, _, strip_rows, width = in_flight.shape
    tiles = width // LANES
    length = 2 * strip_rows // BLOCKS
    swap = [(0, 1), (1, 0)]
    plane = PLANE if depth % PLANE == 0 else depth
    ring = [(i, i - i % plane + (i + 1) % plane) for i in range(depth)]

    def crossing(loops):
        ways = {}
        for loop in loops:
            ways.update(zip(loop, (*loop[1:], loop[0])))
        return [(2 * d + c, 2 * ways[d] + c if d in ways else 2 * d + 1 - c) for d in range(depth) for c in range(2)]

    starts = range(plane, depth, plane)
    loops = [(first - 1, first, first - 3) for first in starts]
    later = [(first - 1, first, first + 2) for first in starts]
    if loops:
        loops.append((depth - 2, depth - 1))
        later += [(0, 1), *((first + 1, first + 1 + plane) for first in starts[:-1:2])]
    cross = {1: crossing(loops), 2: crossing(later)}
    blocks = f32(2, length, tiles, BLOCKS, LANES)
    window = f32(2, tiles, strip_rows + 2 * MARGIN, LANES)
    natural = pltpu.VMEM((tiles, 2 * BLOCKS * length + 2 * PAD, LANES), jnp.float32)
    scratch = field_scratch(length, tiles) + [natural]
    strips = f32(3, strip_rows, width)
    flops = 20 * TERMS * 4 * strip_rows * width

    loads = [pltpu.VMEM((strip_rows, width), jnp.int32), pltpu.SemaphoreType.DMA((2,))]
    (send,) = call(split_kernel, [strips], [HBM, HBM], loads, in_hbm(in_flight, classes))
    got = lax.ppermute(send, "lat", swap)
    freq_phase, in_flight, _ = lax.optimization_barrier((freq_phase, in_flight, send))
    (own,) = call(
        weave_kernel,
        [f32(3, tiles, strip_rows, LANES)],
        [HBM, HBM],
        [pltpu.VMEM(strips.shape, jnp.float32), *loads],
        in_hbm(in_flight, classes),
    )
    table = coefficients(freq_phase, class_slowness)
    hand, over, cells = call(
        first_kernel,
        [blocks, blocks, jax.ShapeDtypeStruct(blocks.shape[1:], jnp.int32)],
        [VMEM, VMEM, VMEM, VMEM],
        scratch,
        (own, got, table, entering),
        flops,
    )
    mines, sent, coefficient = [], (), {}
    for turn in range(1, TURNS):
        handed = lax.ppermute(hand, "depth", ring)
        crossed = lax.ppermute(over, ("depth", "lat"), cross[min(turn, 2)])
        if turn == 1:
            entered = crossed
        mine, send = call(
            window_kernel,
            [window, f32(turn, *window.shape)],
            [VMEM] * (1 + len(sent)),
            [natural],
            (hand, *sent),
        )
        mines.append(mine)
        if turn == 1:
            for later in range(1, TURNS):
                (coefficient[later],) = call(
                    functools.partial(coefficient_kernel, later),
                    [f32(TERMS, *blocks.shape[1:])],
                    [VMEM] * 2,
                    [],
                    (cells, table),
                )
            coefficient[1], send, *others = lax.optimization_barrier(
                (coefficient[1], send, *(coefficient[later] for later in range(2, TURNS)))
            )
            coefficient.update(zip(range(2, TURNS), others))
        sent = (send,)
        last = turn == TURNS - 1
        outs = call(
            functools.partial(next_kernel, turn, plane),
            [blocks, window] if last else [blocks],
            [VMEM] * 5,
            scratch,
            (handed, crossed, entered, coefficient[turn], entering),
            flops,
        )
        hand = over = outs[0]
    earlier = lax.ppermute(send, "lat", swap)
    hand, send = outs
    got = lax.ppermute(send, "lat", swap)
    (mine,) = call(own_window_kernel, [window], [VMEM], [natural], (hand,))
    (early,) = call(
        early_kernel,
        [f32(OFFSETS, tiles, strip_rows, LANES)],
        [VMEM] * TURNS,
        [],
        (*mines, earlier),
    )
    return tuple(
        call(
            image_kernel,
            [f32(1, OFFSETS, strip_rows, width), f32(1, 4, strip_rows, width)],
            [VMEM] * 3,
            [
                pltpu.VMEM((tiles, OFFSETS, strip_rows, LANES), jnp.float32),
                pltpu.VMEM((4, strip_rows, width), jnp.float32),
                pltpu.SemaphoreType.DMA((1 + tiles,)),
            ],
            (early, mine, got),
            out_specs=[HBM] * 2,
        )
    )


def inside_kernel(turn, limits_ref, field_ref, blocks_ref, table_ref, out_ref, a, b):
    a[...] = field_ref[...]
    side = lax.axis_index("lat") % 2
    valid = (limits_ref[0], limits_ref[1])
    advance(a, b, out_ref, looked_up(blocks_ref, table_ref, turn, side), valid)


def grouped(in_flight, entering, classes, freq_phase, class_slowness):
    depth, strips = lax.axis_size("depth"), lax.axis_size("lat")
    strip = lax.axis_index("lat")
    side, group = strip % 2, strip // 2
    _, _, strip_rows, width = in_flight.shape
    tiles = width // LANES
    core = 2 * strip_rows
    halo = TERMS - 1 + MARGIN
    while (core + 2 * halo) % BLOCKS:
        halo += 1
    rows = core + 2 * halo
    length = rows // BLOCKS
    swap = [(i, i ^ 1) for i in range(strips)]
    shift = [(i, i + 1) for i in range(depth - 1)]
    blocks = f32(2, length, tiles, BLOCKS, LANES)

    def both_strips(mine, sent):
        got = lax.ppermute(sent, "lat", swap)
        return jnp.where(
            side == 0, jnp.concatenate([mine, got], 1), jnp.concatenate([got, mine], 1)
        )

    def own_components(fields):
        return both_strips(
            lax.dynamic_slice_in_dim(fields, 2 * side, 2, 0),
            lax.dynamic_slice_in_dim(fields, 2 * (1 - side), 2, 0),
        )

    def with_halo(cells):
        above = lax.ppermute(cells[:, core - halo :], "lat", [(i, i + 2) for i in range(strips - 2)])
        below = lax.ppermute(cells[:, :halo], "lat", [(i + 2, i) for i in range(strips - 2)])
        return jnp.concatenate([above, cells, below], 1)

    def to_blocks(cells):
        split = cells.reshape(-1, BLOCKS, length, LANES, tiles)
        return split.transpose(0, 2, 4, 1, 3)

    def to_rows(cells):
        return cells.transpose(0, 3, 1, 4, 2).reshape(2, rows, width)

    def window(cells, which):
        begin = halo - MARGIN + which * strip_rows
        return lax.dynamic_slice_in_dim(cells, begin, strip_rows + 2 * MARGIN, 1)

    cells = to_blocks(with_halo(both_strips(classes, classes)))[0]
    table = coefficients(freq_phase, class_slowness)
    before = group * core - halo
    limits = jnp.stack([jnp.maximum(-before, 0), jnp.minimum(strips * strip_rows - before, rows)])
    field = own_components(in_flight[0])
    images = jnp.zeros((OFFSETS, strip_rows, width), jnp.float32)
    for turn in range(TURNS):
        (advanced,) = call(
            functools.partial(inside_kernel, turn),
            [blocks],
            [SMEM, VMEM, VMEM, VMEM],
            field_scratch(length, tiles),
            (limits.astype(jnp.int32), to_blocks(with_halo(field)), cells, table),
        )
        advanced = to_rows(advanced)
        mine = window(advanced, side)
        got = lax.ppermute(window(advanced, 1 - side), "lat", swap)
        source, receiver = jnp.where(side == 0, mine, got), jnp.where(side == 0, got, mine)
        products = []
        for o in range(OFFSETS):
            lag = o - MARGIN
            first = source[:, MARGIN - lag : MARGIN - lag + strip_rows]
            second = receiver[:, MARGIN + lag : MARGIN + lag + strip_rows]
            products.append(first[0] * second[0] + first[1] * second[1])
        images = images + jnp.stack(products)
        if turn + 1 < TURNS:
            handed = lax.ppermute(advanced[:, halo : halo + core], "depth", shift)
            entered = own_components(entering[turn])
            field = jnp.where(lax.axis_index("depth") == 0, entered, handed)
    own = slice(MARGIN, MARGIN + strip_rows)
    return images[None], jnp.concatenate([source[:, own], receiver[:, own]], 0)[None]


def solution(mesh):
    in_specs = (
        P("depth", None, "lat", None),
        P(None, None, "lat", None),
        P("depth", "lat", None),
        P(),
        P(),
    )
    out_specs = (P("depth", None, "lat", None), P("depth", None, "lat", None))
    pair = mesh.shape["lat"] == 2
    local = paired if pair else grouped
    return jax.shard_map(local, mesh=mesh, in_specs=in_specs, out_specs=out_specs, check_vma=False)
```
